32 devices in a mesh: ens: 2 (over y), space: 4 (over z), tm: 2 (over x), spin: 2 (over core).
Axes of the slice: x: 2, y: 2, z: 4, core: 2. Of those that a mesh axis runs over, the one named last changes fastest.
Arguments:
- eigvecs: bfloat16 [4, 2, 3, 8192, 128], P('tm', None, None, 'space'), may hold values from -6 to 6
- links: bfloat16 [4, 3, 2, 3, 3, 8192], P('tm', None, None, None, None, 'space'), may hold values from -2.5 to 2.5
- directions: int32 [4], P('spin'), may hold values from 0 to 3, each once
- pair_list: int32 [32, 2], P(('space', 'tm')), may hold values from 0 to 3
- pair_operators: int32 [32, 2], P(('space', 'tm')), may hold values from 0 to 3
- perambulators: bfloat16 [32, 16, 2, 128, 128], P(('space', 'tm'), 'spin'), may hold values from -0.5 to 0.5
Outputs:
- elementals: float32 [8, 4, 128, 2, 128], P(('ens', 'tm'), 'spin', 'space'), parts along dimension 0
- correlators: float32 [64, 2], P(('ens', 'space', 'tm')), parts along dimension 0
The draws below stay inside these ranges and needn't reach their ends.
There are 2 independent parts, one for each index of `ens`. The reference program is written for one: setup_inputs(seed, part) draws one part's arguments, and reference() takes and returns one part's arrays. A program takes and returns all parts, laid end to end along the dimension named above; an argument that names none is the same for every part. Nothing has to cross between parts.
Inputs may be any that keep to these rules, and one draw needn't show every extreme that they name: `directions`: each code once; 0, 1, 2 name a covariant derivative along the first, second and third spatial direction, 3 the eigenvectors with one unit of momentum along the third.
All inputs are finite; a program needn't handle non-finite values.
Results may differ from the reference program's by a relative error of at most 0.0071.
Values may be sent and summed in bfloat16 or wider, within the bound.
A program may use at most 128 MiB of HBM per device.

```python
import math
from functools import partial
import jax
import jax.numpy as jnp
from jax import lax

NEV = 128
SPIN_PAIRS = 16
NOPS = 4
PX = 16
PY = 16
ZB = 8
NT = 4
NSITES = 8192
NP = 32
N_SPACE = 4


def touch_ends(entries, stream_key, low, top_value):
    longest = entries.shape.index(max(entries.shape))
    spots = []
    for shift in (0, 1):
        where = [jax.random.randint(jax.random.fold_in(stream_key, axis), (), 0, length) for axis, length in enumerate(entries.shape)]
        where[longest] = (where[longest] + shift) % entries.shape[longest]
        spots.append(tuple(where))
    return entries.at[spots[0]].set(low).at[spots[1]].set(top_value)


def level_of(stream_key, shape, shards, smallest, top_value):
    def one(dim, blocks):
        draws = jax.random.uniform(jax.random.fold_in(jax.random.fold_in(stream_key, 6), dim), (blocks,), jnp.float32, smallest / len(shards), top_value / len(shards))
        return jnp.repeat(jnp.exp(draws), shape[dim] // blocks).reshape((-1,) + (1,) * (len(shape) - dim - 1))

    level = one(*shards[0])
    for cut in shards[1:]:
        level = level * one(*cut)
    return level


def centred(key, extent, width, reach, shards=(), held_as=jnp.bfloat16):
    loudness = level_of(key, extent, shards, -0.22, 0.18) if shards else 1.0
    entries = jax.random.normal(key, extent, jnp.float32) * width * loudness
    return jnp.minimum(jnp.maximum(entries, -reach), reach).astype(held_as)


def setup_inputs(seed: int = 0, part: int = 0) -> dict:
    seeds = jax.random.split(jax.random.key(seed), 7)
    return {
        "eigvecs": centred(seeds[0], (NT, 2, 3, NSITES, NEV), 1.0, 6.0, ((0, 2), (3, 4))),
        "links": centred(seeds[1], (NT, 3, 2, 3, 3, NSITES), 0.4, 2.5, ((0, 2), (5, 4))),
        "directions": jax.random.permutation(seeds[2], NOPS).astype(jnp.int32),
        "pair_list": touch_ends(jax.random.randint(seeds[3], (NP, 2), 0, NT), jax.random.fold_in(seeds[3], 1), 0, NT - 1).astype(jnp.int32),
        "pair_operators": touch_ends(jax.random.randint(seeds[4], (NP, 2), 0, NOPS), jax.random.fold_in(seeds[4], 1), 0, NOPS - 1).astype(jnp.int32),
        "perambulators": centred(seeds[5], (NP, SPIN_PAIRS, 2, NEV, NEV), NEV ** -0.5, 0.5, ((0, 8), (1, 2))),
    }


def apply_links(link_field, vectors):
    for b in range(3):
        link_real = link_field[0, :, b][..., None]
        link_imag = link_field[1, :, b][..., None]
        term_real = link_real * vectors[0, b] - link_imag * vectors[1, b]
        term_imag = link_real * vectors[1, b] + link_imag * vectors[0, b]
        if b == 0:
            total_real, total_imag = (term_real, term_imag)
        else:
            total_real, total_imag = (total_real + term_real, total_imag + term_imag)
    return jnp.stack([total_real, total_imag])

def apply_adjoint(link_field, vectors):
    for b in range(3):
        link_real = link_field[0, b][..., None]
        link_imag = link_field[1, b][..., None]
        term_real = link_real * vectors[0, b] + link_imag * vectors[1, b]
        term_imag = link_real * vectors[1, b] - link_imag * vectors[0, b]
        if b == 0:
            total_real, total_imag = (term_real, term_imag)
        else:
            total_real, total_imag = (total_real + term_real, total_imag + term_imag)
    return jnp.stack([total_real, total_imag])

def phase_field(vectors, z_coord, z_total):
    angles = 2.0 * math.pi / z_total * z_coord
    cosine_part = jnp.cos(angles)[:, None, None, None]
    sine_part = jnp.sin(angles)[:, None, None, None]
    return jnp.stack([cosine_part * vectors[0] + sine_part * vectors[1], cosine_part * vectors[1] - sine_part * vectors[0]])

def covariant(direction, vectors, link_field):
    roll_axis = 4 - direction
    links_along = link_field[direction]
    forward = apply_links(links_along, jnp.roll(vectors, -1, roll_axis))
    backward = jnp.roll(apply_adjoint(links_along, vectors), 1, roll_axis)
    return 0.5 * (forward - backward)

def gram_block(vectors_half, displaced, scaling):
    columns = vectors_half.shape[-1]
    left_side = vectors_half.reshape(-1, columns)
    displaced_half = displaced.astype(jnp.bfloat16)
    field_real = displaced_half[0].reshape(-1, columns)
    field_imag = displaced_half[1].reshape(-1, columns)
    right_side = jnp.concatenate([jnp.concatenate([field_real, field_imag], 0), jnp.concatenate([field_imag, -field_real], 0)], 1)
    product = lax.dot_general(left_side, right_side, (((0,), (0,)), ((), ())), preferred_element_type=jnp.float32)
    return (product * scaling).reshape(columns, 2, columns)

def contract_pair(source, sink_matrix, blocks, pair_signs):
    columns = source.shape[-1]
    sink_block = jnp.concatenate([jnp.concatenate([sink_matrix[:, 0], -sink_matrix[:, 1]], 1), jnp.concatenate([sink_matrix[:, 1], sink_matrix[:, 0]], 1)], 0)
    source_block = jnp.concatenate([jnp.concatenate([source[:, 0], source[:, 1]], 1), jnp.concatenate([-source[:, 1], source[:, 0]], 1)], 0)
    source_block = source_block.reshape(2, columns, 2 * columns)
    stacked = blocks.reshape(blocks.shape[0], 2 * columns, columns)
    halfway = jnp.einsum('mk,qkn->qmn', sink_block.astype(jnp.float32), stacked.astype(jnp.float32)).astype(jnp.bfloat16)
    second = jnp.einsum('qcmk,ckn->qmn', halfway.reshape(-1, 2, columns, columns).astype(jnp.float32), source_block.astype(jnp.float32))
    tau_real = blocks[:, 0].astype(jnp.float32)
    tau_imag = blocks[:, 1].astype(jnp.float32)
    out_real = second[:, :, :columns]
    out_imag = second[:, :, columns:]
    trace_real = lax.optimization_barrier(jnp.sum(out_real * tau_real + out_imag * tau_imag, axis=(1, 2)))
    trace_imag = lax.optimization_barrier(jnp.sum(out_imag * tau_real - out_real * tau_imag, axis=(1, 2)))
    return jnp.stack([jnp.sum(pair_signs * trace_real), jnp.sum(pair_signs * trace_imag)]) / (4.0 * columns)

def reference(eigvecs, links, directions, pair_list, pair_operators, perambulators):
    z_total = ZB * N_SPACE
    scaling = 1.0 / math.sqrt(6.0 * PX * PY * z_total)
    z_coord = jnp.arange(z_total).astype(jnp.float32)
    branches = [partial(covariant, 0), partial(covariant, 1), partial(covariant, 2), lambda vectors, link_field: phase_field(vectors, z_coord, z_total)]

    def per_slice(inputs):
        vectors_half, link_half = inputs
        vectors = vectors_half.astype(jnp.float32).reshape(2, 3, z_total, PY, PX, NEV)
        link_field = link_half.astype(jnp.float32).reshape(3, 2, 3, 3, z_total, PY, PX)
        blocks = []
        for op_slot in range(NOPS):
            displaced = lax.switch(directions[op_slot], branches, vectors, link_field)
            blocks.append(gram_block(vectors_half, displaced, scaling))
        return jnp.stack(blocks)
    elementals = lax.map(per_slice, (eigvecs, links))
    halves = elementals.astype(jnp.bfloat16)
    spin_signs = jnp.where(jnp.arange(4) < 2, 1.0, -1.0).astype(jnp.float32)
    pair_signs = (spin_signs[:, None] * spin_signs[None, :]).reshape(SPIN_PAIRS)

    def per_pair(inputs):
        time_pair, operator_pair, blocks = inputs
        source = halves[time_pair[0], operator_pair[0]]
        sink_matrix = halves[time_pair[1], operator_pair[1]]
        return contract_pair(source, sink_matrix, blocks, pair_signs)
    correlators = lax.map(per_pair, (pair_list, pair_operators, perambulators))
    return (elementals, correlators)
```

```python
import functools
import math

import jax
import jax.numpy as jnp
import numpy as np
from jax import lax
from jax.experimental import pallas as pl
from jax.experimental.pallas import tpu as pltpu
from jax.sharding import PartitionSpec as P

PX = 16
PY = 16
PLANE = PX * PY
STRIDE = PY + 1
BF = jnp.bfloat16
F32 = jnp.float32
LANES = 128
MESH = pl.DeviceIdType.MESH


def fill_links(lk, links, phases, t, first_plane, plane_count):
    for code in range(3):
        for b in range(3):
            for a in range(3):
                pair = links[t, code, b, a].astype(F32)
                for part in range(2):
                    lk[code, pl.ds(part * 9 + b * 3 + a, 1), :] = pair[part : part + 1]
    for plane in range(plane_count):
        lanes = pl.ds(plane * PLANE, PLANE)
        entries = [phases[0, first_plane + plane], -phases[1, first_plane + plane]]
        for part in range(2):
            for b in range(3):
                for a in range(3):
                    value = entries[part] if a == b else 0.0
                    lk[3, pl.ds(part * 9 + b * 3 + a, 1), lanes] = jnp.full((1, PLANE), value, F32)


def stage_plane(work, turned, vin, t, plane, plane_count):
    last = lax.broadcasted_iota(jnp.int32, (8, work.shape[-1]), 0) == 7
    source = plane * PLANE
    moved = (plane_count + 1) * STRIDE

    def group(g, carry):
        for part in range(2):
            for a in range(3):
                value = vin[t, part, a, pl.ds(pl.multiple_of(source + g * PX, PX), PX), :]
                work[part, a, plane * STRIDE + g] = value
                wide = value.astype(F32)
                low, high = pltpu.roll(wide[:8], 7, 0), pltpu.roll(wide[8:], 7, 0)
                shifted = jnp.concatenate(
                    [jnp.where(last, high, low), jnp.where(last, low, high)], axis=0
                )
                work[part, a, moved + plane * STRIDE + g] = shifted.astype(BF)
        return carry

    lax.fori_loop(0, PY, group, 0, unroll=2)
    for part in range(2):
        for a in range(3):
            edge = vin[t, part, a, pl.ds(pl.multiple_of(source, PX), PX), :]
            work[part, a, plane * STRIDE + PY] = edge
            for s in range(PLANE // LANES):
                at = pl.ds(pl.multiple_of(source + s * LANES, LANES), LANES)
                turned[part, a, plane * (PLANE // LANES) + s] = vin[t, part, a, at, :].T


def link_product(turned, lk, product, code, group, place):
    rows = 16
    columns = turned.shape[-2]
    lanes = pl.ds(pl.multiple_of(group * LANES, LANES), LANES)

    def link(part, b, a):
        return jnp.broadcast_to(lk[code, pl.ds(part * 9 + b * 3 + a, 1), lanes], (rows, LANES))

    u = [[[link(part, b, a) for a in range(3)] for b in range(3)] for part in range(2)]
    for first in range(0, columns, rows):
        real = [turned[0, b, group, pl.ds(first, rows), :].astype(F32) for b in range(3)]
        imag = [turned[1, b, group, pl.ds(first, rows), :].astype(F32) for b in range(3)]
        for a in range(3):
            out_real = out_imag = None
            for b in range(3):
                ur, ui = u[0][b][a], u[1][b][a]
                term_real = ur * real[b] + ui * imag[b]
                term_imag = ur * imag[b] - ui * real[b]
                out_real = term_real if b == 0 else out_real + term_real
                out_imag = term_imag if b == 0 else out_imag + term_imag
            product[a, place, pl.ds(first, rows), :] = out_real.astype(BF)
            product[a, place, pl.ds(columns + first, rows), :] = out_imag.astype(BF)


def gram(product, work, first, chunk, offset):
    total = None
    for s in range(chunk):
        lines = [(first + s) * STRIDE + y + offset for y in range(PY)]
        for a in range(3):
            left = jnp.concatenate([product[a, 2 * s], product[a, 2 * s + 1]], axis=1)
            right = jnp.concatenate(
                [
                    jnp.concatenate([work[part, a, line] for line in lines], axis=0)
                    for part in range(2)
                ],
                axis=1,
            )
            term = jnp.dot(left, right, preferred_element_type=F32)
            total = term if total is None else total + term
    return total


def contract(sink, source, tau, p, spin_signs, columns):
    sr, si = sink[:, :columns], sink[:, columns:]
    sink_block = jnp.concatenate(
        [jnp.concatenate([sr, -si], axis=1), jnp.concatenate([si, sr], axis=1)], axis=0
    )
    rr, ri = source[:, :columns], source[:, columns:]
    source_block = jnp.concatenate(
        [jnp.concatenate([rr, ri], axis=1), jnp.concatenate([-ri, rr], axis=1)], axis=0
    )
    total_real = jnp.zeros((8, columns), F32)
    total_imag = jnp.zeros((8, columns), F32)
    count = tau.shape[1]
    for first in range(0, count, 2):
        some = range(first, min(first + 2, count))
        stacked = jnp.concatenate(
            [jnp.concatenate([tau[p, q, 0], tau[p, q, 1]], axis=0) for q in some], axis=1
        )
        halfway = jnp.dot(sink_block, stacked, preferred_element_type=F32).astype(BF)
        lines = jnp.concatenate(
            [
                jnp.concatenate(
                    [
                        halfway[:columns, n * columns : (n + 1) * columns],
                        halfway[columns:, n * columns : (n + 1) * columns],
                    ],
                    axis=1,
                )
                for n in range(len(some))
            ],
            axis=0,
        )
        second = jnp.dot(lines, source_block, preferred_element_type=F32)
        for n, q in enumerate(some):
            out_real = second[n * columns : (n + 1) * columns, :columns]
            out_imag = second[n * columns : (n + 1) * columns, columns:]
            tau_real = tau[p, q, 0].astype(F32)
            tau_imag = tau[p, q, 1].astype(F32)
            real = out_real * tau_real + out_imag * tau_imag
            imag = out_imag * tau_real - out_real * tau_imag
            total_real += spin_signs[q] * jnp.sum(real.reshape(-1, 8, columns), axis=0)
            total_imag += spin_signs[q] * jnp.sum(imag.reshape(-1, 8, columns), axis=0)
    return total_real, total_imag


def meson_kernel(
    sizes,
    chunk,
    scaling,
    dirs,
    pair_times,
    pair_ops,
    phases,
    v_hbm,
    links_hbm,
    tau_hbm,
    e_out,
    c_out,
    vin,
    links,
    tau,
    halo,
    work,
    lk,
    turned,
    product,
    acc,
    own,
    held,
    table,
    partial,
    v_sem,
    links_sem,
    tau_sem,
    halo_send,
    halo_recv,
    relay_send,
    relay_recv,
    r_send,
    r_recv,
    z_send,
    z_recv,
    t_send,
    t_recv,
    c_send,
    c_recv,
    p_send,
    p_recv,
):
    layers, times, cores = sizes["space"], sizes["tm"], sizes["spin"]
    here = {axis: lax.axis_index(axis) for axis in sizes}
    slices, _, _, local_sites, columns = vin.shape
    ops = dirs.shape[0]
    plane_count = local_sites // PLANE
    chunks = plane_count // chunk
    rows = columns // layers
    units = slices * ops

    def local(src, dst, sem):
        return pltpu.make_async_copy(src, dst, sem)

    def remote(src, dst, send, recv, axis, distance):
        target = lax.rem(here[axis] + distance, sizes[axis])
        return pltpu.make_async_remote_copy(
            src_ref=src,
            dst_ref=dst,
            send_sem=send,
            recv_sem=recv,
            device_id={axis: target},
            device_id_type=MESH,
        )

    def plane_copy(t, z):
        at = pl.ds(pl.multiple_of(z * PLANE, PLANE), PLANE)
        return local(v_hbm.at[t, :, :, at, :], vin.at[t, :, :, at, :], v_sem.at[t, z])

    links_copy = local(links_hbm, links, links_sem)
    tau_copy = local(tau_hbm, tau, tau_sem)

    links_copy.start()
    for t in range(slices):
        for z in range(plane_count):
            plane_copy(t, z).start()

    barrier = pltpu.get_barrier_semaphore()
    for axis, size in sizes.items():
        for d in range(1, size):
            pl.semaphore_signal(
                barrier,
                inc=1,
                device_id={axis: lax.rem(here[axis] + d, size)},
                device_id_type=MESH,
            )
    pl.semaphore_wait(barrier, layers + times + cores - 3)

    core = here["spin"]

    def halo_copy(t):
        return remote(
            v_hbm.at[t, core, :, pl.ds(0, PLANE), :],
            halo.at[t, core],
            halo_send.at[t],
            halo_recv.at[t],
            "space",
            layers - 1,
        )

    def relay_copy(t):
        return remote(
            halo.at[t, core], halo.at[t, core], relay_send.at[t], relay_recv.at[t], "spin", 1
        )

    for t in range(slices):
        halo_copy(t).start()
    tau_copy.start()
    links_copy.wait()

    def reduce_copy(u, d):
        peer = lax.rem(here["space"] + d, layers)
        return remote(
            own.at[u, peer], held.at[u, d - 1], r_send.at[u, d], r_recv.at[u, d], "space", d
        )

    def finish_unit(u):
        code = dirs[u % ops]
        value = acc[...]
        real = value[:columns, :columns] + value[columns:, columns:]
        imag = value[:columns, columns:] - value[columns:, :columns]
        straight = jnp.where(code == 3, scaling, 0.5 * scaling)
        crossed = jnp.where(code == 3, 0.0, 0.5 * scaling)
        whole = jnp.concatenate(
            [straight * real - crossed * real.T, straight * imag + crossed * imag.T], axis=1
        )
        own[u] = whole.reshape(layers, rows, 2 * columns)
        for d in range(1, layers):
            reduce_copy(u, d).start()

    def slot(u, d, e):
        z = lax.rem(here["space"] + layers - d, layers)
        x = lax.rem(here["tm"] + times - e, times)
        return table.at[z, x, core, u]

    def z_copy(u, d):
        return remote(slot(u, 0, 0), slot(u, 0, 0), z_send.at[u, d], z_recv.at[u, d], "space", d)

    def t_copy(u, d, e):
        block = slot(u, d, 0)
        return remote(block, block, t_send.at[u, d, e], t_recv.at[u, d, e], "tm", e)

    def c_copy(u, d, e):
        block = slot(u, d, e)
        return remote(block, block, c_send.at[u, d, e], c_recv.at[u, d, e], "spin", 1)

    def pass_on(u, d):
        for e in range(1, times):
            t_copy(u, d, e).start()
        c_copy(u, d, 0).start()

    def reduce_unit(u):
        total = own[u, here["space"]]
        for d in range(1, layers):
            reduce_copy(u, d).wait_recv()
            total += held[u, d - 1]
        for part in range(2):
            e_out[u // ops, u % ops, :, part, :] = total[:, part * columns : (part + 1) * columns]
        table[here["space"], here["tm"], core, u] = total.astype(BF)
        for d in range(1, layers):
            z_copy(u, d).start()
        pass_on(u, 0)

    def spread_layers(u):
        for d in range(1, layers):
            z_copy(u, d).wait_recv()
            pass_on(u, d)

    def spread_times(u):
        for d in range(layers):
            for e in range(1, times):
                t_copy(u, d, e).wait_recv()
                c_copy(u, d, e).start()

    def step(i, carry):
        u, n = i // chunks, lax.rem(i, chunks)
        t, o = u // ops, lax.rem(u, ops)
        first = n * chunk

        @pl.when(n == 0)
        def _():
            acc[...] = jnp.zeros_like(acc)

        @pl.when(o == 0)
        def _():
            @pl.when(n == 0)
            def _():
                fill_links(lk, links, phases, t, here["space"] * plane_count, plane_count)

            def stage(plane, carry):
                plane_copy(t, plane).wait()
                stage_plane(work, turned, vin, t, plane, plane_count)
                return carry

            low = jnp.where(n == 0, 0, first + 1)
            high = jnp.minimum(first + chunk + 1, plane_count)
            lax.fori_loop(low, high, stage, 0)

        for which in range(units):
            base = which * chunks
            if which % ops == 0:
                when = which // ops

                @pl.when(i == base + chunks - 2)
                def _():
                    halo_copy(when).wait_recv()
                    relay_copy(when).start()

                @pl.when(i == base + chunks - 1)
                def _():
                    relay_copy(when).wait_recv()
                    for part in range(2):
                        for a in range(3):
                            for y in range(PY):
                                line = halo[when, part, a, pl.ds(y * PX, PX), :]
                                work[part, a, plane_count * STRIDE + y] = line

            if which > 0:

                @pl.when(i == base + chunks - 3)
                def _():
                    reduce_unit(which - 1)

                @pl.when(i == base + chunks - 2)
                def _():
                    spread_layers(which - 1)

                @pl.when(i == base + chunks - 1)
                def _():
                    spread_times(which - 1)

        code = dirs[o]
        offset = jnp.where(
            code == 0,
            (plane_count + 1) * STRIDE,
            jnp.where(code == 1, 1, jnp.where(code == 2, STRIDE, 0)),
        )
        groups = chunk * (PLANE // LANES)
        for s in range(groups):
            link_product(turned, lk, product, code, n * groups + s, s)
        acc[...] += gram(product, work, first, chunk, offset)

        for which in range(units - 1):

            @pl.when(i == which * chunks + chunks - 1)
            def _():
                finish_unit(which)

        return carry

    lax.fori_loop(0, units * chunks, step, 0)
    last = units - 1
    finish_unit(last)
    reduce_unit(last)
    spread_layers(last)
    spread_times(last)
    tau_copy.wait()
    for u in range(units):
        for d in range(layers):
            for e in range(times):
                c_copy(u, d, e).wait_recv()

    count = tau.shape[1]
    spin_signs = []
    for q in range(count):
        pair = core * count + q
        same = (pair // 4 < 2) == (lax.rem(pair, 4) < 2)
        spin_signs.append(jnp.where(same, 1.0, -1.0))

    def entry(which, p):
        time, op = pair_times[which, p], pair_ops[which, p]
        block = table[
            :,
            lax.div(time, slices),
            lax.div(op, ops),
            lax.rem(time, slices) * ops + lax.rem(op, ops),
        ]
        return block.astype(F32).reshape(columns, 2 * columns).astype(BF)

    pair_count = tau.shape[0]

    def one_pair(p, carry):
        total_real, total_imag = contract(
            entry(1, p), entry(0, p), tau, p, spin_signs, columns
        )
        partial[0, 0, p] = total_real
        partial[0, 1, p] = total_imag
        return carry

    lax.fori_loop(0, pair_count, one_pair, 0)
    p_copy = remote(partial.at[0], partial.at[1], p_send, p_recv, "spin", 1)
    p_copy.start()
    p_copy.wait_recv()
    for part in range(2):
        for p in range(pair_count):
            both = partial[0, part, p] + partial[1, part, p]
            c_out[part, p] = jnp.sum(both) / (4.0 * columns)

    p_copy.wait_send()
    for t in range(slices):
        halo_copy(t).wait_send()
        relay_copy(t).wait_send()
    for u in range(units):
        for d in range(1, layers):
            reduce_copy(u, d).wait_send()
            z_copy(u, d).wait_send()
        for d in range(layers):
            for e in range(times):
                if e:
                    t_copy(u, d, e).wait_send()
                c_copy(u, d, e).wait_send()


def shards(eigvecs, links, directions, pair_list, pair_operators, perambulators):
    slices, _, _, local_sites, columns = eigvecs.shape
    sizes = {axis: lax.axis_size(axis) for axis in ("space", "tm", "spin")}
    layers, times, cores = sizes["space"], sizes["tm"], sizes["spin"]
    plane_count = local_sites // PLANE
    z_total = plane_count * layers
    scaling = 1.0 / math.sqrt(6.0 * PLANE * z_total)
    ops = directions.shape[0]
    rows = columns // layers
    pair_count = pair_list.shape[0]
    chunk = 2
    units = slices * ops
    angles = 2.0 * np.pi / z_total * np.arange(z_total)
    phases = jnp.asarray(np.stack([np.cos(angles), np.sin(angles)]), F32)

    dma = pltpu.SemaphoreType.DMA
    vmem = pl.BlockSpec(memory_space=pltpu.VMEM)
    smem = pl.BlockSpec(memory_space=pltpu.SMEM)
    anywhere = pl.BlockSpec(memory_space=pl.ANY)
    by_link = jnp.transpose(links, (0, 1, 3, 4, 2, 5))
    elementals, correlators = pl.pallas_call(
        functools.partial(meson_kernel, sizes, chunk, scaling),
        out_shape=(
            jax.ShapeDtypeStruct((slices, ops, rows, 2, columns), F32),
            jax.ShapeDtypeStruct((2, pair_count), F32),
        ),
        in_specs=[smem, smem, smem, smem, anywhere, anywhere, anywhere],
        out_specs=(vmem, smem),
        scratch_shapes=[
            pltpu.VMEM(eigvecs.shape, BF),
            pltpu.VMEM(by_link.shape, BF),
            pltpu.VMEM(perambulators.shape, BF),
            pltpu.VMEM((slices, 2, 3, PLANE, columns), BF),
            pltpu.VMEM((2, 3, (2 * plane_count + 1) * STRIDE, PX, columns), BF),
            pltpu.VMEM((4, 18, local_sites), F32),
            pltpu.VMEM((2, 3, local_sites // LANES, columns, LANES), BF),
            pltpu.VMEM((3, chunk * PLANE // LANES, 2 * columns, LANES), BF),
            pltpu.VMEM((2 * columns, 2 * columns), F32),
            pltpu.VMEM((units, layers, rows, 2 * columns), F32),
            pltpu.VMEM((units, layers - 1, rows, 2 * columns), F32),
            pltpu.VMEM((layers, times, cores, units, rows, 2 * columns), BF),
            pltpu.VMEM((2, 2, pair_count, 8, columns), F32),
            dma((slices, plane_count)),
            dma(()),
            dma(()),
            dma((slices,)),
            dma((slices,)),
            dma((slices,)),
            dma((slices,)),
            dma((units, layers)),
            dma((units, layers)),
            dma((units, layers)),
            dma((units, layers)),
            dma((units, layers, times)),
            dma((units, layers, times)),
            dma((units, layers, times)),
            dma((units, layers, times)),
            dma(()),
            dma(()),
        ],
        compiler_params=pltpu.CompilerParams(
            collective_id=0, has_side_effects=True, vmem_limit_bytes=56 << 20
        ),
        cost_estimate=pl.CostEstimate(
            flops=5_000_000_000, bytes_accessed=eigvecs.size * 2, transcendentals=0
        ),
        name="meson",
    )(directions, pair_list.T, pair_operators.T, phases, eigvecs, by_link, perambulators)
    return elementals, correlators.T


def solution(mesh):
    return jax.shard_map(
        shards,
        mesh=mesh,
        in_specs=(
            P("tm", None, None, "space", None),
            P("tm", None, None, None, None, "space"),
            P("spin"),
            P(("space", "tm"), None),
            P(("space", "tm"), None),
            P(("space", "tm"), "spin", None, None, None),
        ),
        out_specs=(P(("ens", "tm"), "spin", "space", None, None), P(("ens", "space", "tm"), None)),
        check_vma=False,
    )
```

```python
import functools
import math

import jax
import jax.numpy as jnp
import numpy as np
from jax import lax
from jax.experimental import pallas as pl
from jax.experimental.pallas import tpu as pltpu
from jax.sharding import PartitionSpec as P

PX = 16
PY = 16
PLANE = PX * PY
BF = jnp.bfloat16
F32 = jnp.float32
LANES = 128
WAIT = 3
MESH = pl.DeviceIdType.MESH


def fill_links(lk, links, phases, t, first_plane, plane_count):
    def keep(code, b, a, lanes, real, imag):
        for kind, value in enumerate((real, imag - real, imag + real)):
            lk[code, pl.ds(kind * 9 + b * 3 + a, 1), lanes] = value

    for code in range(3):
        for b in range(3):
            for a in range(3):
                pair = links[t, code, b, a].astype(F32)
                keep(code, b, a, slice(None), pair[0:1], pair[1:2])
    for plane in range(plane_count):
        lanes = pl.ds(plane * PLANE, PLANE)
        for b in range(3):
            for a in range(3):
                real = phases[0, first_plane + plane] if a == b else 0.0
                imag = -phases[1, first_plane + plane] if a == b else 0.0
                keep(
                    3, b, a, lanes, jnp.full((1, PLANE), real, F32), jnp.full((1, PLANE), imag, F32)
                )


def stage_plane(work, turned, vin, t, plane, plane_count):
    last = lax.broadcasted_iota(jnp.int32, (8, work.shape[-1]), 0) == 7
    source = plane * PLANE
    along_y, along_x = plane_count + 1 + plane, 2 * plane_count + 1 + plane

    def group(g, carry):
        here = pl.ds(pl.multiple_of(g * PX, PX), PX)
        before = pl.ds(pl.multiple_of(lax.rem(g + PY - 1, PY) * PX, PX), PX)
        for part in range(2):
            for a in range(3):
                value = vin[t, part, a, pl.ds(pl.multiple_of(source + g * PX, PX), PX), :]
                work[part, a, plane, here, :] = value
                work[part, a, along_y, before, :] = value
                wide = value.astype(F32)
                low, high = pltpu.roll(wide[:8], 7, 0), pltpu.roll(wide[8:], 7, 0)
                shifted = jnp.concatenate(
                    [jnp.where(last, high, low), jnp.where(last, low, high)], axis=0
                )
                work[part, a, along_x, here, :] = shifted.astype(BF)
        return carry

    lax.fori_loop(0, PY, group, 0, unroll=2)
    for part in range(2):
        for a in range(3):
            for s in range(PLANE // LANES):
                at = pl.ds(pl.multiple_of(source + s * LANES, LANES), LANES)
                turned[part, a, plane * (PLANE // LANES) + s] = vin[t, part, a, at, :].T


def link_product(turned, lk, product, code, group, place):
    rows = 16
    columns = turned.shape[-2]
    lanes = pl.ds(pl.multiple_of(group * LANES, LANES), LANES)

    def link(kind, b, a):
        return jnp.broadcast_to(lk[code, pl.ds(kind * 9 + b * 3 + a, 1), lanes], (rows, LANES))

    u = [[[link(kind, b, a) for a in range(3)] for b in range(3)] for kind in range(3)]
    for first in range(0, columns, rows):
        real = [turned[0, b, group, pl.ds(first, rows), :].astype(F32) for b in range(3)]
        imag = [turned[1, b, group, pl.ds(first, rows), :].astype(F32) for b in range(3)]
        both = [real[b] + imag[b] for b in range(3)]

        def row(kind, a, field):
            return (
                u[kind][0][a] * field[0] + u[kind][1][a] * field[1] + u[kind][2][a] * field[2]
            )

        for a in range(3):
            common = row(0, a, both)
            out_real = common + row(1, a, imag)
            out_imag = common - row(2, a, real)
            product[a, place, pl.ds(first, rows), :] = out_real.astype(BF)
            product[a, place, pl.ds(columns + first, rows), :] = out_imag.astype(BF)


def gram(product, work, first, chunk, offset):
    total = None
    for s in range(chunk):
        line = first + s + offset
        for a in range(3):
            left = jnp.concatenate([product[a, 2 * s], product[a, 2 * s + 1]], axis=1)
            right = jnp.concatenate([work[0, a, line], work[1, a, line]], axis=1)
            term = jnp.dot(left, right, preferred_element_type=F32)
            total = term if total is None else total + term
    return total


def contract(sink, source, tau, p, spin_signs, columns):
    sr, si = sink[:, :columns], sink[:, columns:]
    sink_block = jnp.concatenate(
        [jnp.concatenate([sr, -si], axis=1), jnp.concatenate([si, sr], axis=1)], axis=0
    )
    rr, ri = source[:, :columns], source[:, columns:]
    source_block = jnp.concatenate(
        [jnp.concatenate([rr, ri], axis=1), jnp.concatenate([-ri, rr], axis=1)], axis=0
    )
    total_real = jnp.zeros((8, columns), F32)
    total_imag = jnp.zeros((8, columns), F32)
    count = tau.shape[1]
    for first in range(0, count, 2):
        some = range(first, min(first + 2, count))
        stacked = jnp.concatenate(
            [jnp.concatenate([tau[p, q, 0], tau[p, q, 1]], axis=0) for q in some], axis=1
        )
        halfway = jnp.dot(sink_block, stacked, preferred_element_type=F32).astype(BF)
        lines = jnp.concatenate(
            [
                jnp.concatenate(
                    [
                        halfway[:columns, n * columns : (n + 1) * columns],
                        halfway[columns:, n * columns : (n + 1) * columns],
                    ],
                    axis=1,
                )
                for n in range(len(some))
            ],
            axis=0,
        )
        second = jnp.dot(lines, source_block, preferred_element_type=F32)
        for n, q in enumerate(some):
            out_real = second[n * columns : (n + 1) * columns, :columns]
            out_imag = second[n * columns : (n + 1) * columns, columns:]
            tau_real = tau[p, q, 0].astype(F32)
            tau_imag = tau[p, q, 1].astype(F32)
            real = out_real * tau_real + out_imag * tau_imag
            imag = out_imag * tau_real - out_real * tau_imag
            total_real += spin_signs[q] * jnp.sum(real.reshape(-1, 8, columns), axis=0)
            total_imag += spin_signs[q] * jnp.sum(imag.reshape(-1, 8, columns), axis=0)
    return total_real, total_imag


def meson_kernel(
    sizes,
    chunk,
    scaling,
    dirs,
    pair_times,
    pair_ops,
    phases,
    v_hbm,
    links_hbm,
    tau_hbm,
    e_out,
    c_out,
    vin,
    links,
    tau,
    halo,
    work,
    lk,
    turned,
    product,
    acc,
    own,
    held,
    table,
    partial,
    v_sem,
    links_sem,
    tau_sem,
    halo_send,
    halo_recv,
    relay_send,
    relay_recv,
    r_send,
    r_recv,
    z_send,
    z_recv,
    t_send,
    t_recv,
    c_send,
    c_recv,
    p_send,
    p_recv,
):
    layers, times, cores = sizes["space"], sizes["tm"], sizes["spin"]
    here = {axis: lax.axis_index(axis) for axis in sizes}
    slices, _, _, local_sites, columns = vin.shape
    ops = dirs.shape[0]
    plane_count = local_sites // PLANE
    chunks = plane_count // chunk
    rows = columns // layers
    units = slices * ops

    def local(src, dst, sem):
        return pltpu.make_async_copy(src, dst, sem)

    def target(**moves):
        return {axis: lax.rem(here[axis] + d, sizes[axis]) for axis, d in moves.items()}

    def remote(src, dst, send, recv, **moves):
        return pltpu.make_async_remote_copy(
            src_ref=src,
            dst_ref=dst,
            send_sem=send,
            recv_sem=recv,
            device_id=target(**moves),
            device_id_type=MESH,
        )

    def plane_copy(t, z):
        at = pl.ds(pl.multiple_of(z * PLANE, PLANE), PLANE)
        return local(v_hbm.at[t, :, :, at, :], vin.at[t, :, :, at, :], v_sem.at[t, z])

    links_copy = local(links_hbm, links, links_sem)
    tau_copy = local(tau_hbm, tau, tau_sem)

    links_copy.start()
    for t in range(slices):
        for z in range(plane_count):
            plane_copy(t, z).start()

    barrier = pltpu.get_barrier_semaphore()
    for d, e in [(d, e) for d in range(layers) for e in range(times) if d or e]:
        pl.semaphore_signal(
            barrier, inc=1, device_id=target(space=d, tm=e), device_id_type=MESH
        )
    for f in range(1, cores):
        pl.semaphore_signal(barrier, inc=1, device_id=target(spin=f), device_id_type=MESH)
    pl.semaphore_wait(barrier, layers * times + cores - 2)

    core = here["spin"]

    def halo_copy(t):
        return remote(
            v_hbm.at[t, core, :, pl.ds(0, PLANE), :],
            halo.at[t, core],
            halo_send.at[t],
            halo_recv.at[t],
            space=layers - 1,
        )

    def relay_copy(t):
        return remote(
            halo.at[t, core], halo.at[t, core], relay_send.at[t], relay_recv.at[t], spin=1
        )

    for t in range(slices):
        halo_copy(t).start()
    tau_copy.start()
    links_copy.wait()

    def reduce_copy(u, d):
        peer = lax.rem(here["space"] + d, layers)
        return remote(
            own.at[u, peer], held.at[u, d - 1], r_send.at[u, d], r_recv.at[u, d], space=d
        )

    def finish_unit(u):
        code = dirs[u % ops]
        value = acc[u % ops]
        real = value[:columns, :columns] + value[columns:, columns:]
        imag = value[:columns, columns:] - value[columns:, :columns]
        straight = jnp.where(code == 3, scaling, 0.5 * scaling)
        crossed = jnp.where(code == 3, 0.0, 0.5 * scaling)
        whole = jnp.concatenate(
            [straight * real - crossed * real.T, straight * imag + crossed * imag.T], axis=1
        )
        own[u] = whole.reshape(layers, rows, 2 * columns)
        for d in range(1, layers):
            reduce_copy(u, d).start()

    def slot(u, d, e):
        z = lax.rem(here["space"] + layers - d, layers)
        x = lax.rem(here["tm"] + times - e, times)
        return table.at[z, x, core, u]

    def z_copy(u, d):
        return remote(slot(u, 0, 0), slot(u, 0, 0), z_send.at[u, d], z_recv.at[u, d], space=d)

    def t_copy(u, d, e):
        sems = t_send.at[u, d, e], t_recv.at[u, d, e]
        if u == units - 1:
            return remote(slot(u, 0, 0), slot(u, 0, 0), *sems, space=d, tm=e)
        return remote(slot(u, d, 0), slot(u, d, 0), *sems, tm=e)

    def c_copy(u, d, e):
        block = slot(u, d, e)
        return remote(block, block, c_send.at[u, d, e], c_recv.at[u, d, e], spin=1)

    def start_times(u, d):
        for e in range(1, times):
            t_copy(u, d, e).start()

    def reduce_unit(u):
        total = own[u, here["space"]]
        for d in range(1, layers):
            reduce_copy(u, d).wait_recv()
            total += held[u, d - 1]
        e_out[u // ops, u % ops] = total
        table[here["space"], here["tm"], core, u] = total.astype(BF)
        for d in range(1, layers):
            z_copy(u, d).start()
        for d in range(layers if u == units - 1 else 1):
            start_times(u, d)
        c_copy(u, 0, 0).start()

    def spread_layers(u):
        for d in range(1, layers):
            z_copy(u, d).wait_recv()
            if u < units - 1:
                start_times(u, d)
            c_copy(u, d, 0).start()

    def spread_times(u):
        for d in range(layers):
            for e in range(1, times):
                t_copy(u, d, e).wait_recv()
                c_copy(u, d, e).start()

    total_steps = units * chunks
    inner = ops * (chunks - 1)

    def fetch_halo(t):
        halo_copy(t).wait_recv()
        relay_copy(t).start()

    def place_halo(t):
        relay_copy(t).wait_recv()
        for part in range(2):
            for a in range(3):
                work[part, a, plane_count] = halo[t, part, a]

    events = []
    for t in range(slices):
        needed = inner if t == 0 else t * ops * chunks + chunks - 1
        events += [(needed - 1, fetch_halo, t), (needed, place_halo, t)]
    for u in range(units):
        done = inner + u if u < ops else (u + 1) * chunks - 1
        events += [(done + 1, finish_unit, u), (done + 1 + WAIT, reduce_unit, u)]
        events += [(done + 1 + 2 * WAIT, spread_layers, u)]
        events += [(done + 1 + (2 if u == units - 1 else 3) * WAIT, spread_times, u)]
    events.sort(key=lambda event: event[0])

    def step(i, carry):
        for when, action, which in events:
            if when < total_steps:

                @pl.when(i == when)
                def _(action=action, which=which):
                    action(which)

        head = i < ops * chunks
        plain = lax.rem(i // chunks, ops)
        o = jnp.where(head, jnp.where(i < inner, i // (chunks - 1), i - inner), plain)
        n = jnp.where(
            head, jnp.where(i < inner, lax.rem(i, chunks - 1), chunks - 1), lax.rem(i, chunks)
        )
        t = i // (ops * chunks)
        first = n * chunk

        @pl.when(o == 0)
        def _():
            @pl.when(n == 0)
            def _():
                fill_links(lk, links, phases, t, here["space"] * plane_count, plane_count)

            def stage(plane, carry):
                plane_copy(t, plane).wait()
                stage_plane(work, turned, vin, t, plane, plane_count)
                return carry

            low = jnp.where(n == 0, 0, first + 1)
            high = jnp.minimum(first + chunk + 1, plane_count)
            lax.fori_loop(low, high, stage, 0)

        code = dirs[o]
        offset = jnp.where(
            code == 0,
            2 * plane_count + 1,
            jnp.where(code == 1, plane_count + 1, jnp.where(code == 2, 1, 0)),
        )
        groups = chunk * (PLANE // LANES)
        for s in range(groups):
            link_product(turned, lk, product, code, n * groups + s, s)
        term = gram(product, work, first, chunk, offset)

        @pl.when(n == 0)
        def _():
            acc[o] = term

        @pl.when(n > 0)
        def _():
            acc[o] += term

        return carry

    lax.fori_loop(0, total_steps, step, 0)
    for when, action, which in events:
        if when >= total_steps:
            action(which)
    tau_copy.wait()
    for u in range(units):
        for d in range(layers):
            for e in range(times):
                c_copy(u, d, e).wait_recv()

    count = tau.shape[1]
    spin_signs = []
    for q in range(count):
        pair = core * count + q
        same = (pair // 4 < 2) == (lax.rem(pair, 4) < 2)
        spin_signs.append(jnp.where(same, 1.0, -1.0))

    def entry(which, p):
        time, op = pair_times[which, p], pair_ops[which, p]
        block = table[
            :,
            lax.div(time, slices),
            lax.div(op, ops),
            lax.rem(time, slices) * ops + lax.rem(op, ops),
        ]
        return block.astype(F32).reshape(columns, 2 * columns).astype(BF)

    pair_count = tau.shape[0]

    def one_pair(p, carry):
        total_real, total_imag = contract(
            entry(1, p), entry(0, p), tau, p, spin_signs, columns
        )
        partial[0, 0, pl.ds(p, 1), :] = jnp.sum(total_real, axis=0, keepdims=True)
        partial[0, 1, pl.ds(p, 1), :] = jnp.sum(total_imag, axis=0, keepdims=True)
        return carry

    lax.fori_loop(0, pair_count, one_pair, 0)
    p_copy = remote(partial.at[0], partial.at[1], p_send, p_recv, spin=1)
    p_copy.start()
    p_copy.wait_recv()
    c_out[...] = partial[0] + partial[1]
    p_copy.wait_send()
    for t in range(slices):
        halo_copy(t).wait_send()
        relay_copy(t).wait_send()
    for u in range(units):
        for d in range(1, layers):
            reduce_copy(u, d).wait_send()
            z_copy(u, d).wait_send()
        for d in range(layers):
            for e in range(times):
                if e:
                    t_copy(u, d, e).wait_send()
                c_copy(u, d, e).wait_send()


def last_kernel(blocks, sums, e_out, c_out):
    columns = e_out.shape[-1]
    for part in range(2):
        e_out[:, :, :, part, :] = blocks[:, :, :, part * columns : (part + 1) * columns]
        for p in range(sums.shape[1]):
            c_out[part, p] = jnp.sum(sums[part, p]) / (4.0 * columns)


def shards(eigvecs, links, directions, pair_list, pair_operators, perambulators):
    slices, _, _, local_sites, columns = eigvecs.shape
    sizes = {axis: lax.axis_size(axis) for axis in ("space", "tm", "spin")}
    layers, times, cores = sizes["space"], sizes["tm"], sizes["spin"]
    plane_count = local_sites // PLANE
    z_total = plane_count * layers
    scaling = 1.0 / math.sqrt(6.0 * PLANE * z_total)
    ops = directions.shape[0]
    rows = columns // layers
    pair_count = pair_list.shape[0]
    chunk = 2
    units = slices * ops
    angles = 2.0 * np.pi / z_total * np.arange(z_total)
    phases = jnp.asarray(np.stack([np.cos(angles), np.sin(angles)]), F32)

    dma = pltpu.SemaphoreType.DMA
    vmem = pl.BlockSpec(memory_space=pltpu.VMEM)
    smem = pl.BlockSpec(memory_space=pltpu.SMEM)
    anywhere = pl.BlockSpec(memory_space=pl.ANY)
    by_link = jnp.transpose(links, (0, 1, 3, 4, 2, 5))
    blocks, sums = pl.pallas_call(
        functools.partial(meson_kernel, sizes, chunk, scaling),
        out_shape=(
            jax.ShapeDtypeStruct((slices, ops, rows, 2 * columns), F32),
            jax.ShapeDtypeStruct((2, pair_count, columns), F32),
        ),
        in_specs=[smem, smem, smem, smem, anywhere, anywhere, anywhere],
        out_specs=(vmem, vmem),
        scratch_shapes=[
            pltpu.VMEM(eigvecs.shape, BF),
            pltpu.VMEM(by_link.shape, BF),
            pltpu.VMEM(perambulators.shape, BF),
            pltpu.VMEM((slices, 2, 3, PLANE, columns), BF),
            pltpu.VMEM((2, 3, 3 * plane_count + 1, PLANE, columns), BF),
            pltpu.VMEM((4, 27, local_sites), F32),
            pltpu.VMEM((2, 3, local_sites // LANES, columns, LANES), BF),
            pltpu.VMEM((3, chunk * PLANE // LANES, 2 * columns, LANES), BF),
            pltpu.VMEM((ops, 2 * columns, 2 * columns), F32),
            pltpu.VMEM((units, layers, rows, 2 * columns), F32),
            pltpu.VMEM((units, layers - 1, rows, 2 * columns), F32),
            pltpu.VMEM((layers, times, cores, units, rows, 2 * columns), BF),
            pltpu.VMEM((2, 2, pair_count, columns), F32),
            dma((slices, plane_count)),
            dma(()),
            dma(()),
            dma((slices,)),
            dma((slices,)),
            dma((slices,)),
            dma((slices,)),
            dma((units, layers)),
            dma((units, layers)),
            dma((units, layers)),
            dma((units, layers)),
            dma((units, layers, times)),
            dma((units, layers, times)),
            dma((units, layers, times)),
            dma((units, layers, times)),
            dma(()),
            dma(()),
        ],
        compiler_params=pltpu.CompilerParams(
            collective_id=0, has_side_effects=True, vmem_limit_bytes=56 << 20
        ),
        cost_estimate=pl.CostEstimate(
            flops=5_000_000_000, bytes_accessed=eigvecs.size * 2, transcendentals=0
        ),
        name="meson",
    )(directions, pair_list.T, pair_operators.T, phases, eigvecs, by_link, perambulators)
    elementals, correlators = pl.pallas_call(
        last_kernel,
        out_shape=(
            jax.ShapeDtypeStruct((slices, ops, rows, 2, columns), F32),
            jax.ShapeDtypeStruct((2, pair_count), F32),
        ),
        in_specs=[vmem, vmem],
        out_specs=(vmem, smem),
        name="last",
    )(blocks, sums)
    return elementals, correlators.T


def solution(mesh):
    return jax.shard_map(
        shards,
        mesh=mesh,
        in_specs=(
            P("tm", None, None, "space", None),
            P("tm", None, None, None, None, "space"),
            P("spin"),
            P(("space", "tm"), None),
            P(("space", "tm"), None),
            P(("space", "tm"), "spin", None, None, None),
        ),
        out_specs=(P(("ens", "tm"), "spin", "space", None, None), P(("ens", "space", "tm"), None)),
        check_vma=False,
    )
```

```python
import functools
import math

import jax
import jax.numpy as jnp
import numpy as np
from jax import lax
from jax.experimental import pallas as pl
from jax.experimental.pallas import tpu as pltpu
from jax.sharding import PartitionSpec as P

PX = 16
PY = 16
PLANE = PX * PY
BF = jnp.bfloat16
F32 = jnp.float32
LANES = 128
WAIT = 6
MESH = pl.DeviceIdType.MESH


def fill_links(lk, links, phases, t, first_plane, plane_count):
    def keep(code, b, a, lanes, real, imag):
        for kind, value in enumerate((real, imag - real, imag + real)):
            lk[code, pl.ds(kind * 9 + b * 3 + a, 1), lanes] = value

    for code in range(3):
        for b in range(3):
            for a in range(3):
                pair = links[t, code, b, a].astype(F32)
                keep(code, b, a, slice(None), pair[0:1], pair[1:2])
    for plane in range(plane_count):
        lanes = pl.ds(plane * PLANE, PLANE)
        for b in range(3):
            for a in range(3):
                real = phases[0, first_plane + plane] if a == b else 0.0
                imag = -phases[1, first_plane + plane] if a == b else 0.0
                keep(
                    3, b, a, lanes, jnp.full((1, PLANE), real, F32), jnp.full((1, PLANE), imag, F32)
                )


def stage_plane(work, turned, plane, plane_count):
    last = lax.broadcasted_iota(jnp.int32, (8, work.shape[-1]), 0) == 7
    along_x = 2 * plane_count + 1 + plane

    def group(g, carry):
        here = pl.ds(pl.multiple_of(g * PX, PX), PX)
        for part in range(2):
            for a in range(3):
                wide = work[part, a, plane, here, :].astype(F32)
                low, high = pltpu.roll(wide[:8], 7, 0), pltpu.roll(wide[8:], 7, 0)
                shifted = jnp.concatenate(
                    [jnp.where(last, high, low), jnp.where(last, low, high)], axis=0
                )
                work[part, a, along_x, here, :] = shifted.astype(BF)
        return carry

    lax.fori_loop(0, PY, group, 0, unroll=True)
    for part in range(2):
        for a in range(3):
            for s in range(PLANE // LANES):
                at = pl.ds(s * LANES, LANES)
                turned[part, a, plane * (PLANE // LANES) + s] = work[part, a, plane, at, :].T


def link_product(turned, lk, product, code, group):
    rows = 16
    columns = turned.shape[-2]
    lanes = pl.ds(pl.multiple_of(group * LANES, LANES), LANES)

    def link(kind, b, a):
        return jnp.broadcast_to(lk[code, pl.ds(kind * 9 + b * 3 + a, 1), lanes], (rows, LANES))

    u = [[[link(kind, b, a) for a in range(3)] for b in range(3)] for kind in range(3)]
    for first in range(0, columns, rows):
        real = [turned[0, b, group, pl.ds(first, rows), :].astype(F32) for b in range(3)]
        imag = [turned[1, b, group, pl.ds(first, rows), :].astype(F32) for b in range(3)]
        both = [real[b] + imag[b] for b in range(3)]

        def row(kind, a, field):
            return (
                u[kind][0][a] * field[0] + u[kind][1][a] * field[1] + u[kind][2][a] * field[2]
            )

        for a in range(3):
            common = row(0, a, both)
            out_real = common + row(1, a, imag)
            out_imag = common - row(2, a, real)
            product[a, group, pl.ds(first, rows), :] = out_real.astype(BF)
            product[a, group, pl.ds(columns + first, rows), :] = out_imag.astype(BF)


def gram(product, work, plane_count, offset):
    total = None
    for a in range(3):
        left = jnp.concatenate([product[a, s] for s in range(product.shape[1])], axis=1)
        right = jnp.concatenate(
            [
                jnp.concatenate([work[0, a, z + offset], work[1, a, z + offset]], axis=1)
                for z in range(plane_count)
            ],
            axis=0,
        )
        term = jnp.dot(left, right, preferred_element_type=F32)
        total = term if total is None else total + term
    return total


def contract(sink, source, tau, p, spin_signs, columns):
    sr, si = sink[:, :columns], sink[:, columns:]
    sink_block = jnp.concatenate(
        [jnp.concatenate([sr, -si], axis=1), jnp.concatenate([si, sr], axis=1)], axis=0
    )
    rr, ri = source[:, :columns], source[:, columns:]
    source_block = jnp.concatenate(
        [jnp.concatenate([rr, ri], axis=1), jnp.concatenate([-ri, rr], axis=1)], axis=0
    )
    total_real = jnp.zeros((8, columns), F32)
    total_imag = jnp.zeros((8, columns), F32)
    count = tau.shape[1]
    for first in range(0, count, 2):
        some = range(first, min(first + 2, count))
        stacked = jnp.concatenate(
            [jnp.concatenate([tau[p, q, 0], tau[p, q, 1]], axis=0) for q in some], axis=1
        )
        halfway = jnp.dot(sink_block, stacked, preferred_element_type=F32).astype(BF)
        lines = jnp.concatenate(
            [
                jnp.concatenate(
                    [
                        halfway[:columns, n * columns : (n + 1) * columns],
                        halfway[columns:, n * columns : (n + 1) * columns],
                    ],
                    axis=1,
                )
                for n in range(len(some))
            ],
            axis=0,
        )
        second = jnp.dot(lines, source_block, preferred_element_type=F32)
        for n, q in enumerate(some):
            out_real = second[n * columns : (n + 1) * columns, :columns]
            out_imag = second[n * columns : (n + 1) * columns, columns:]
            tau_real = tau[p, q, 0].astype(F32)
            tau_imag = tau[p, q, 1].astype(F32)
            real = out_real * tau_real + out_imag * tau_imag
            imag = out_imag * tau_real - out_real * tau_imag
            total_real += spin_signs[q] * jnp.sum(real.reshape(-1, 8, columns), axis=0)
            total_imag += spin_signs[q] * jnp.sum(imag.reshape(-1, 8, columns), axis=0)
    return total_real, total_imag


def meson_kernel(sizes, slices, scaling, *refs):
    dirs, pair_times, pair_ops, phases, v_hbm, links_hbm, tau_hbm, e_out, c_out = refs[:9]
    works = refs[9 : 9 + slices]
    products = refs[9 + slices : 9 + slices + dirs.shape[0]]
    links, tau, lk, turned, own, held, table, partial = refs[9 + slices + dirs.shape[0] :][:8]
    (
        v_sem,
        y_sem,
        links_sem,
        tau_sem,
        halo_send,
        halo_recv,
        relay_send,
        relay_recv,
        r_send,
        r_recv,
        z_send,
        z_recv,
        t_send,
        t_recv,
        c_send,
        c_recv,
        p_send,
        p_recv,
    ) = refs[17 + slices + dirs.shape[0] :]
    layers, times, cores = sizes["space"], sizes["tm"], sizes["spin"]
    here = {axis: lax.axis_index(axis) for axis in sizes}
    plane_count, columns = v_hbm.shape[3], v_hbm.shape[5]
    ops = dirs.shape[0]
    groups = plane_count * (PLANE // LANES)
    rows = columns // layers
    units = slices * ops

    def local(src, dst, sem):
        return pltpu.make_async_copy(src, dst, sem)

    def target(**moves):
        return {axis: lax.rem(here[axis] + d, sizes[axis]) for axis, d in moves.items()}

    def remote(src, dst, send, recv, **moves):
        return pltpu.make_async_remote_copy(
            src_ref=src,
            dst_ref=dst,
            send_sem=send,
            recv_sem=recv,
            device_id=target(**moves),
            device_id_type=MESH,
        )

    def plane_copy(t, z):
        return local(v_hbm.at[t, :, :, z], works[t].at[:, :, z], v_sem.at[t, z])

    def y_copies(t):
        planes = pl.ds(plane_count + 1, plane_count)
        inner, edge = PLANE - PX, pl.ds(PLANE - PX, PX)
        return [
            local(
                v_hbm.at[t, :, :, :, pl.ds(PX, inner), :],
                works[t].at[:, :, planes, pl.ds(0, inner), :],
                y_sem.at[t, 0],
            ),
            local(
                v_hbm.at[t, :, :, :, pl.ds(0, PX), :],
                works[t].at[:, :, planes, edge, :],
                y_sem.at[t, 1],
            ),
        ]

    links_copy = local(links_hbm, links, links_sem)
    tau_copy = local(tau_hbm, tau, tau_sem)

    for z in range(plane_count):
        plane_copy(0, z).start()
    links_copy.start()

    barrier = pltpu.get_barrier_semaphore()
    for d, e in [(d, e) for d in range(layers) for e in range(times) if d or e]:
        pl.semaphore_signal(
            barrier, inc=1, device_id=target(space=d, tm=e), device_id_type=MESH
        )
    for f in range(1, cores):
        pl.semaphore_signal(barrier, inc=1, device_id=target(spin=f), device_id_type=MESH)
    pl.semaphore_wait(barrier, layers * times + cores - 2)

    core = here["spin"]

    def halo_copy(t):
        return remote(
            v_hbm.at[t, core, :, 0],
            works[t].at[core, :, plane_count],
            halo_send.at[t],
            halo_recv.at[t],
            space=layers - 1,
        )

    def relay_copy(t):
        plane = works[t].at[core, :, plane_count]
        return remote(plane, plane, relay_send.at[t], relay_recv.at[t], spin=1)

    for t in range(slices):
        halo_copy(t).start()
    for copy in y_copies(0):
        copy.start()
    for t in range(1, slices):
        for z in range(plane_count):
            plane_copy(t, z).start()
        for copy in y_copies(t):
            copy.start()
    tau_copy.start()

    def reduce_copy(u, d):
        peer = lax.rem(here["space"] + d, layers)
        return remote(
            own.at[u, peer], held.at[u, d - 1], r_send.at[u, d], r_recv.at[u, d], space=d
        )

    def finish_unit(u):
        code = dirs[u % ops]
        offset = jnp.where(
            code == 0,
            2 * plane_count + 1,
            jnp.where(code == 1, plane_count + 1, jnp.where(code == 2, 1, 0)),
        )
        value = gram(products[u % ops], works[u // ops], plane_count, offset)
        real = value[:columns, :columns] + value[columns:, columns:]
        imag = value[:columns, columns:] - value[columns:, :columns]
        straight = jnp.where(code == 3, scaling, 0.5 * scaling)
        crossed = jnp.where(code == 3, 0.0, 0.5 * scaling)
        whole = jnp.concatenate(
            [straight * real - crossed * real.T, straight * imag + crossed * imag.T], axis=1
        )
        own[u] = whole.reshape(layers, rows, 2 * columns)
        for d in range(1, layers):
            reduce_copy(u, d).start()

    def slot(u, d, e):
        z = lax.rem(here["space"] + layers - d, layers)
        x = lax.rem(here["tm"] + times - e, times)
        return table.at[z, x, core, u]

    def z_copy(u, d):
        return remote(slot(u, 0, 0), slot(u, 0, 0), z_send.at[u, d], z_recv.at[u, d], space=d)

    def t_copy(u, d, e):
        sems = t_send.at[u, d, e], t_recv.at[u, d, e]
        if u == units - 1:
            return remote(slot(u, 0, 0), slot(u, 0, 0), *sems, space=d, tm=e)
        return remote(slot(u, d, 0), slot(u, d, 0), *sems, tm=e)

    def c_copy(u, d, e):
        block = slot(u, d, e)
        return remote(block, block, c_send.at[u, d, e], c_recv.at[u, d, e], spin=1)

    def start_times(u, d):
        for e in range(1, times):
            t_copy(u, d, e).start()

    def reduce_unit(u):
        total = own[u, here["space"]]
        for d in range(1, layers):
            reduce_copy(u, d).wait_recv()
            total += held[u, d - 1]
        e_out[u // ops, u % ops] = total
        table[here["space"], here["tm"], core, u] = total.astype(BF)
        for d in range(1, layers):
            z_copy(u, d).start()
        for d in range(layers if u == units - 1 else 1):
            start_times(u, d)
        c_copy(u, 0, 0).start()

    def spread_layers(u):
        for d in range(1, layers):
            z_copy(u, d).wait_recv()
            if u < units - 1:
                start_times(u, d)
            c_copy(u, d, 0).start()

    def spread_times(u):
        for d in range(layers):
            for e in range(1, times):
                t_copy(u, d, e).wait_recv()
                c_copy(u, d, e).start()

    pending = []

    def tick():
        for entry in list(pending):
            entry[0] -= 1
            if entry[0] == 0:
                pending.remove(entry)
                entry[1](entry[2])

    def fetch_halo(t):
        halo_copy(t).wait_recv()
        relay_copy(t).start()

    def whole_slice(t):
        relay_copy(t).wait_recv()
        for copy in y_copies(t):
            copy.wait()

    def stage_slice(t):
        def stage(plane, carry):
            plane_copy(t, plane).wait()
            stage_plane(works[t], turned, plane, plane_count)
            return carry

        for half in range(2):
            lax.fori_loop(half * plane_count // 2, (half + 1) * plane_count // 2, stage, 0)
            tick()
        if t == 0:
            links_copy.wait()
        fill_links(lk, links, phases, t, here["space"] * plane_count, plane_count)

    def link_unit(u):
        def group(g, carry):
            link_product(turned, lk, products[u % ops], dirs[u % ops], g)
            return carry

        for half in range(2):
            lax.fori_loop(half * groups // 2, (half + 1) * groups // 2, group, 0)
            tick()

    def close_unit(u):
        finish_unit(u)
        pending.append([WAIT, reduce_unit, u])
        pending.append([2 * WAIT, spread_layers, u])
        pending.append([(2 if u == units - 1 else 3) * WAIT, spread_times, u])
        tick()

    stage_slice(0)
    for t in range(slices):
        first, last = t * ops, (t + 1) * ops - 1
        for u in range(first, last + 1):
            if t == 0 and u == last:
                pending.append([1, fetch_halo, t])
            if t > 0 and u == first:
                pending.append([1, fetch_halo, t])
            link_unit(u)
            if t > 0 and u < last:
                if u == first:
                    whole_slice(t)
                close_unit(u)
        if t == 0:
            whole_slice(t)
            for u in range(first, last):
                close_unit(u)
        if t + 1 < slices:
            stage_slice(t + 1)
        if t > 0 and first == last:
            whole_slice(t)
        close_unit(last)
    while pending:
        tick()
    tau_copy.wait()
    for u in range(units):
        for d in range(layers):
            for e in range(times):
                c_copy(u, d, e).wait_recv()

    count = tau.shape[1]
    spin_signs = []
    for q in range(count):
        pair = core * count + q
        same = (pair // 4 < 2) == (lax.rem(pair, 4) < 2)
        spin_signs.append(jnp.where(same, 1.0, -1.0))

    def entry(which, p):
        time, op = pair_times[which, p], pair_ops[which, p]
        block = table[
            :,
            lax.div(time, slices),
            lax.div(op, ops),
            lax.rem(time, slices) * ops + lax.rem(op, ops),
        ]
        return block.astype(F32).reshape(columns, 2 * columns).astype(BF)

    pair_count = tau.shape[0]

    def one_pair(p, carry):
        total_real, total_imag = contract(
            entry(1, p), entry(0, p), tau, p, spin_signs, columns
        )
        partial[0, 0, pl.ds(p, 1), :] = jnp.sum(total_real, axis=0, keepdims=True)
        partial[0, 1, pl.ds(p, 1), :] = jnp.sum(total_imag, axis=0, keepdims=True)
        return carry

    lax.fori_loop(0, pair_count, one_pair, 0, unroll=True)
    p_copy = remote(partial.at[0], partial.at[1], p_send, p_recv, spin=1)
    p_copy.start()
    p_copy.wait_recv()
    c_out[...] = partial[0] + partial[1]
    p_copy.wait_send()
    for t in range(slices):
        halo_copy(t).wait_send()
        relay_copy(t).wait_send()
    for u in range(units):
        for d in range(1, layers):
            reduce_copy(u, d).wait_send()
            z_copy(u, d).wait_send()
        for d in range(layers):
            for e in range(times):
                if e:
                    t_copy(u, d, e).wait_send()
                c_copy(u, d, e).wait_send()


def last_kernel(blocks, sums, e_out, c_out):
    columns = e_out.shape[-1]
    for part in range(2):
        e_out[:, :, :, part, :] = blocks[:, :, :, part * columns : (part + 1) * columns]
        for p in range(sums.shape[1]):
            c_out[part, p] = jnp.sum(sums[part, p]) / (4.0 * columns)


def shards(eigvecs, links, directions, pair_list, pair_operators, perambulators):
    slices, _, _, local_sites, columns = eigvecs.shape
    sizes = {axis: lax.axis_size(axis) for axis in ("space", "tm", "spin")}
    layers, times, cores = sizes["space"], sizes["tm"], sizes["spin"]
    plane_count = local_sites // PLANE
    z_total = plane_count * layers
    scaling = 1.0 / math.sqrt(6.0 * PLANE * z_total)
    ops = directions.shape[0]
    rows = columns // layers
    pair_count = pair_list.shape[0]
    groups = local_sites // LANES
    units = slices * ops
    angles = 2.0 * np.pi / z_total * np.arange(z_total)
    phases = jnp.asarray(np.stack([np.cos(angles), np.sin(angles)]), F32)

    dma = pltpu.SemaphoreType.DMA
    vmem = pl.BlockSpec(memory_space=pltpu.VMEM)
    smem = pl.BlockSpec(memory_space=pltpu.SMEM)
    anywhere = pl.BlockSpec(memory_space=pl.ANY)
    by_link = jnp.transpose(links, (0, 1, 3, 4, 2, 5))
    by_plane = eigvecs.reshape(slices, 2, 3, plane_count, PLANE, columns)
    blocks, sums = pl.pallas_call(
        functools.partial(meson_kernel, sizes, slices, scaling),
        out_shape=(
            jax.ShapeDtypeStruct((slices, ops, rows, 2 * columns), F32),
            jax.ShapeDtypeStruct((2, pair_count, columns), F32),
        ),
        in_specs=[smem, smem, smem, smem, anywhere, anywhere, anywhere],
        out_specs=(vmem, vmem),
        scratch_shapes=[
            *[pltpu.VMEM((2, 3, 3 * plane_count + 1, PLANE, columns), BF) for _ in range(slices)],
            *[pltpu.VMEM((3, groups, 2 * columns, LANES), BF) for _ in range(ops)],
            pltpu.VMEM(by_link.shape, BF),
            pltpu.VMEM(perambulators.shape, BF),
            pltpu.VMEM((4, 27, local_sites), F32),
            pltpu.VMEM((2, 3, groups, columns, LANES), BF),
            pltpu.VMEM((units, layers, rows, 2 * columns), F32),
            pltpu.VMEM((units, layers - 1, rows, 2 * columns), F32),
            pltpu.VMEM((layers, times, cores, units, rows, 2 * columns), BF),
            pltpu.VMEM((2, 2, pair_count, columns), F32),
            dma((slices, plane_count)),
            dma((slices, 2)),
            dma(()),
            dma(()),
            dma((slices,)),
            dma((slices,)),
            dma((slices,)),
            dma((slices,)),
            dma((units, layers)),
            dma((units, layers)),
            dma((units, layers)),
            dma((units, layers)),
            dma((units, layers, times)),
            dma((units, layers, times)),
            dma((units, layers, times)),
            dma((units, layers, times)),
            dma(()),
            dma(()),
        ],
        compiler_params=pltpu.CompilerParams(
            collective_id=0, has_side_effects=True, vmem_limit_bytes=56 << 20
        ),
        cost_estimate=pl.CostEstimate(
            flops=5_000_000_000, bytes_accessed=eigvecs.size * 2, transcendentals=0
        ),
        name="meson",
    )(directions, pair_list.T, pair_operators.T, phases, by_plane, by_link, perambulators)
    elementals, correlators = pl.pallas_call(
        last_kernel,
        out_shape=(
            jax.ShapeDtypeStruct((slices, ops, rows, 2, columns), F32),
            jax.ShapeDtypeStruct((2, pair_count), F32),
        ),
        in_specs=[vmem, vmem],
        out_specs=(vmem, smem),
        name="last",
    )(blocks, sums)
    return elementals, correlators.T


def solution(mesh):
    return jax.shard_map(
        shards,
        mesh=mesh,
        in_specs=(
            P("tm", None, None, "space", None),
            P("tm", None, None, None, None, "space"),
            P("spin"),
            P(("space", "tm"), None),
            P(("space", "tm"), None),
            P(("space", "tm"), "spin", None, None, None),
        ),
        out_specs=(P(("ens", "tm"), "spin", "space", None, None), P(("ens", "space", "tm"), None)),
        check_vma=False,
    )
```

```python
import functools
import math

import jax
import jax.numpy as jnp
import numpy as np
from jax import lax
from jax.experimental import pallas as pl
from jax.experimental.pallas import tpu as pltpu
from jax.sharding import PartitionSpec as P

PX = 16
PY = 16
PLANE = PX * PY
BF = jnp.bfloat16
F32 = jnp.float32
LANES = 128
WAIT = 6
MESH = pl.DeviceIdType.MESH


def fill_links(lk, links, phases, t, first_plane, plane_count):
    def keep(code, b, a, lanes, real, imag):
        for kind, value in enumerate((real, imag - real, imag + real)):
            lk[code, pl.ds(kind * 9 + b * 3 + a, 1), lanes] = value

    for code in range(3):
        for b in range(3):
            for a in range(3):
                pair = links[t, code, b, a].astype(F32)
                keep(code, b, a, slice(None), pair[0:1], pair[1:2])
    if t > 0:
        return
    for plane in range(plane_count):
        lanes = pl.ds(plane * PLANE, PLANE)
        for b in range(3):
            for a in range(3):
                real = phases[0, first_plane + plane] if a == b else 0.0
                imag = -phases[1, first_plane + plane] if a == b else 0.0
                keep(
                    3, b, a, lanes, jnp.full((1, PLANE), real, F32), jnp.full((1, PLANE), imag, F32)
                )


def stage_plane(work, turned, plane, plane_count):
    last = lax.broadcasted_iota(jnp.int32, (8, work.shape[-1]), 0) == 7
    along_x = 2 * plane_count + 1 + plane

    def group(g, carry):
        here = pl.ds(pl.multiple_of(g * PX, PX), PX)
        for part in range(2):
            for a in range(3):
                wide = work[part, a, plane, here, :].astype(F32)
                low, high = pltpu.roll(wide[:8], 7, 0), pltpu.roll(wide[8:], 7, 0)
                shifted = jnp.concatenate(
                    [jnp.where(last, high, low), jnp.where(last, low, high)], axis=0
                )
                work[part, a, along_x, here, :] = shifted.astype(BF)
        return carry

    lax.fori_loop(0, PY, group, 0, unroll=True)
    for part in range(2):
        for a in range(3):
            for s in range(PLANE // LANES):
                at = pl.ds(s * LANES, LANES)
                turned[part, a, plane * (PLANE // LANES) + s] = work[part, a, plane, at, :].T


def link_product(turned, lk, product, code, group):
    rows = 16
    columns = turned.shape[-2]
    lanes = pl.ds(pl.multiple_of(group * LANES, LANES), LANES)

    def link(kind, b, a):
        return jnp.broadcast_to(lk[code, pl.ds(kind * 9 + b * 3 + a, 1), lanes], (rows, LANES))

    u = [[[link(kind, b, a) for a in range(3)] for b in range(3)] for kind in range(3)]
    for first in range(0, columns, rows):
        real = [turned[0, b, group, pl.ds(first, rows), :].astype(F32) for b in range(3)]
        imag = [turned[1, b, group, pl.ds(first, rows), :].astype(F32) for b in range(3)]
        both = [real[b] + imag[b] for b in range(3)]

        def row(kind, a, field):
            return (
                u[kind][0][a] * field[0] + u[kind][1][a] * field[1] + u[kind][2][a] * field[2]
            )

        for a in range(3):
            common = row(0, a, both)
            out_real = common + row(1, a, imag)
            out_imag = common - row(2, a, real)
            product[a, group, pl.ds(first, rows), :] = out_real.astype(BF)
            product[a, group, pl.ds(columns + first, rows), :] = out_imag.astype(BF)


def gram(product, work, plane_count, offset):
    total = None
    for a in range(3):
        left = jnp.concatenate([product[a, s] for s in range(product.shape[1])], axis=1)
        right = jnp.concatenate(
            [
                jnp.concatenate([work[0, a, z + offset], work[1, a, z + offset]], axis=1)
                for z in range(plane_count)
            ],
            axis=0,
        )
        term = jnp.dot(left, right, preferred_element_type=F32)
        total = term if total is None else total + term
    return total


def contract(sink, source, tau, p, spin_signs, columns):
    sr, si = sink[:, :columns], sink[:, columns:]
    sink_block = jnp.concatenate(
        [jnp.concatenate([sr, -si], axis=1), jnp.concatenate([si, sr], axis=1)], axis=0
    )
    rr, ri = source[:, :columns], source[:, columns:]
    source_block = jnp.concatenate(
        [jnp.concatenate([rr, ri], axis=1), jnp.concatenate([-ri, rr], axis=1)], axis=0
    )
    total_real = jnp.zeros((8, columns), F32)
    total_imag = jnp.zeros((8, columns), F32)
    count = tau.shape[1]
    for first in range(0, count, 2):
        some = range(first, min(first + 2, count))
        stacked = jnp.concatenate(
            [jnp.concatenate([tau[p, q, 0], tau[p, q, 1]], axis=0) for q in some], axis=1
        )
        halfway = jnp.dot(sink_block, stacked, preferred_element_type=F32).astype(BF)
        lines = jnp.concatenate(
            [
                jnp.concatenate(
                    [
                        halfway[:columns, n * columns : (n + 1) * columns],
                        halfway[columns:, n * columns : (n + 1) * columns],
                    ],
                    axis=1,
                )
                for n in range(len(some))
            ],
            axis=0,
        )
        second = jnp.dot(lines, source_block, preferred_element_type=F32)
        for n, q in enumerate(some):
            out_real = second[n * columns : (n + 1) * columns, :columns]
            out_imag = second[n * columns : (n + 1) * columns, columns:]
            tau_real = tau[p, q, 0].astype(F32)
            tau_imag = tau[p, q, 1].astype(F32)
            real = out_real * tau_real + out_imag * tau_imag
            imag = out_imag * tau_real - out_real * tau_imag
            total_real += spin_signs[q] * jnp.sum(real.reshape(-1, 8, columns), axis=0)
            total_imag += spin_signs[q] * jnp.sum(imag.reshape(-1, 8, columns), axis=0)
    return total_real, total_imag


def meson_kernel(sizes, slices, scaling, *refs):
    scalars, (v_hbm, links_hbm, tau_hbm, e_out, c_out) = refs[:4], refs[4:9]
    dirs, pair_times, pair_ops, phases, scalar_sem = refs[-5:]
    works = refs[9 : 9 + slices]
    products = refs[9 + slices : 9 + slices + dirs.shape[0]]
    links, tau, lk, turned, own, held, table, partial = refs[9 + slices + dirs.shape[0] :][:8]
    (
        v_sem,
        y_sem,
        links_sem,
        tau_sem,
        halo_send,
        halo_recv,
        relay_send,
        relay_recv,
        r_send,
        r_recv,
        z_send,
        z_recv,
        t_send,
        t_recv,
        c_send,
        c_recv,
        p_send,
        p_recv,
    ) = refs[17 + slices + dirs.shape[0] : -5]
    layers, times, cores = sizes["space"], sizes["tm"], sizes["spin"]
    here = {axis: lax.axis_index(axis) for axis in sizes}
    plane_count, columns = v_hbm.shape[3], v_hbm.shape[5]
    ops = dirs.shape[0]
    groups = plane_count * (PLANE // LANES)
    rows = columns // layers
    units = slices * ops

    def local(src, dst, sem):
        return pltpu.make_async_copy(src, dst, sem)

    def target(**moves):
        return {axis: lax.rem(here[axis] + d, sizes[axis]) for axis, d in moves.items()}

    def remote(src, dst, send, recv, **moves):
        return pltpu.make_async_remote_copy(
            src_ref=src,
            dst_ref=dst,
            send_sem=send,
            recv_sem=recv,
            device_id=target(**moves),
            device_id_type=MESH,
        )

    def plane_copy(t, z):
        return local(v_hbm.at[t, :, :, z], works[t].at[:, :, z], v_sem.at[t, z])

    def y_copies(t):
        planes = pl.ds(plane_count + 1, plane_count)
        inner, edge = PLANE - PX, pl.ds(PLANE - PX, PX)
        return [
            local(
                v_hbm.at[t, :, :, :, pl.ds(PX, inner), :],
                works[t].at[:, :, planes, pl.ds(0, inner), :],
                y_sem.at[t, 0],
            ),
            local(
                v_hbm.at[t, :, :, :, pl.ds(0, PX), :],
                works[t].at[:, :, planes, edge, :],
                y_sem.at[t, 1],
            ),
        ]

    links_copy = local(links_hbm, links, links_sem)
    tau_copy = local(tau_hbm, tau, tau_sem)

    scalar_copies = [
        local(operand, held_as, scalar_sem.at[k])
        for k, (operand, held_as) in enumerate(zip(scalars, (dirs, pair_times, pair_ops, phases)))
    ]
    for copy in scalar_copies:
        copy.start()
    for z in range(plane_count):
        plane_copy(0, z).start()
    links_copy.start()

    barrier = pltpu.get_barrier_semaphore()
    for d, e in [(d, e) for d in range(layers) for e in range(times) if d or e]:
        pl.semaphore_signal(
            barrier, inc=1, device_id=target(space=d, tm=e), device_id_type=MESH
        )
    for f in range(1, cores):
        pl.semaphore_signal(barrier, inc=1, device_id=target(spin=f), device_id_type=MESH)

    core = here["spin"]

    def halo_copy(t):
        return remote(
            v_hbm.at[t, core, :, 0],
            works[t].at[core, :, plane_count],
            halo_send.at[t],
            halo_recv.at[t],
            space=layers - 1,
        )

    def relay_copy(t):
        plane = works[t].at[core, :, plane_count]
        return remote(plane, plane, relay_send.at[t], relay_recv.at[t], spin=1)

    def open_kernel(_):
        pl.semaphore_wait(barrier, layers * times + cores - 2)
        for t in range(slices):
            halo_copy(t).start()
        for copy in y_copies(0):
            copy.start()
        for t in range(1, slices):
            for z in range(plane_count):
                plane_copy(t, z).start()
            for copy in y_copies(t):
                copy.start()
        tau_copy.start()

    def reduce_copy(u, d):
        peer = lax.rem(here["space"] + d, layers)
        return remote(
            own.at[u, peer], held.at[u, d - 1], r_send.at[u, d], r_recv.at[u, d], space=d
        )

    def finish_unit(u):
        code = dirs[u % ops]
        offset = jnp.where(
            code == 0,
            2 * plane_count + 1,
            jnp.where(code == 1, plane_count + 1, jnp.where(code == 2, 1, 0)),
        )
        value = gram(products[u % ops], works[u // ops], plane_count, offset)
        real = value[:columns, :columns] + value[columns:, columns:]
        imag = value[:columns, columns:] - value[columns:, :columns]
        straight = jnp.where(code == 3, scaling, 0.5 * scaling)
        crossed = jnp.where(code == 3, 0.0, 0.5 * scaling)
        whole = jnp.concatenate(
            [straight * real - crossed * real.T, straight * imag + crossed * imag.T], axis=1
        )
        own[u] = whole.reshape(layers, rows, 2 * columns)
        for d in range(1, layers):
            reduce_copy(u, d).start()

    def slot(u, d, e):
        z = lax.rem(here["space"] + layers - d, layers)
        x = lax.rem(here["tm"] + times - e, times)
        return table.at[z, x, core, u]

    def z_copy(u, d):
        return remote(slot(u, 0, 0), slot(u, 0, 0), z_send.at[u, d], z_recv.at[u, d], space=d)

    def t_copy(u, d, e):
        sems = t_send.at[u, d, e], t_recv.at[u, d, e]
        if u == units - 1:
            return remote(slot(u, 0, 0), slot(u, 0, 0), *sems, space=d, tm=e)
        return remote(slot(u, d, 0), slot(u, d, 0), *sems, tm=e)

    def c_copy(u, d, e):
        block = slot(u, d, e)
        return remote(block, block, c_send.at[u, d, e], c_recv.at[u, d, e], spin=1)

    def start_times(u, d):
        for e in range(1, times):
            t_copy(u, d, e).start()

    def reduce_unit(u):
        total = own[u, here["space"]]
        for d in range(1, layers):
            reduce_copy(u, d).wait_recv()
            total += held[u, d - 1]
        e_out[u // ops, u % ops] = total
        table[here["space"], here["tm"], core, u] = total.astype(BF)
        for d in range(1, layers):
            z_copy(u, d).start()
        for d in range(layers if u == units - 1 else 1):
            start_times(u, d)
        c_copy(u, 0, 0).start()

    def spread_layers(u):
        for d in range(1, layers):
            z_copy(u, d).wait_recv()
            if u < units - 1:
                start_times(u, d)
            c_copy(u, d, 0).start()

    def spread_times(u):
        for d in range(layers):
            for e in range(1, times):
                t_copy(u, d, e).wait_recv()
                c_copy(u, d, e).start()

    pending = []

    def tick():
        for entry in list(pending):
            entry[0] -= 1
            if entry[0] == 0:
                pending.remove(entry)
                entry[1](entry[2])

    def fetch_halo(t):
        halo_copy(t).wait_recv()
        relay_copy(t).start()

    def whole_slice(t):
        relay_copy(t).wait_recv()
        for copy in y_copies(t):
            copy.wait()

    def stage_slice(t):
        def stage(plane, carry):
            plane_copy(t, plane).wait()
            stage_plane(works[t], turned, plane, plane_count)
            return carry

        for half in range(2):
            lax.fori_loop(half * plane_count // 2, (half + 1) * plane_count // 2, stage, 0)
            tick()
        if t == 0:
            for copy in scalar_copies:
                copy.wait()
            links_copy.wait()
        fill_links(lk, links, phases, t, here["space"] * plane_count, plane_count)

    def link_unit(u):
        def group(g, carry):
            link_product(turned, lk, products[u % ops], dirs[u % ops], g)
            return carry

        for half in range(2):
            lax.fori_loop(half * groups // 2, (half + 1) * groups // 2, group, 0)
            tick()

    def close_unit(u):
        finish_unit(u)
        pending.append([WAIT, reduce_unit, u])
        pending.append([2 * WAIT, spread_layers, u])
        pending.append([(2 if u == units - 1 else 3) * WAIT, spread_times, u])
        tick()

    pending.append([1, open_kernel, None])
    stage_slice(0)
    for t in range(slices):
        first, last = t * ops, (t + 1) * ops - 1
        for u in range(first, last + 1):
            if t == 0 and u == last:
                pending.append([1, fetch_halo, t])
            if t > 0 and u == first:
                pending.append([1, fetch_halo, t])
            link_unit(u)
            if t > 0 and u < last:
                if u == first:
                    whole_slice(t)
                close_unit(u)
        if t == 0:
            whole_slice(t)
            for u in range(first, last):
                close_unit(u)
        if t + 1 < slices:
            stage_slice(t + 1)
        if t > 0 and first == last:
            whole_slice(t)
        close_unit(last)
    while pending:
        tick()
    tau_copy.wait()
    for u in range(units):
        for d in range(layers):
            for e in range(times):
                c_copy(u, d, e).wait_recv()

    count = tau.shape[1]
    spin_signs = []
    for q in range(count):
        pair = core * count + q
        same = (pair // 4 < 2) == (lax.rem(pair, 4) < 2)
        spin_signs.append(jnp.where(same, 1.0, -1.0))

    def entry(which, p):
        time, op = pair_times[which, p], pair_ops[which, p]
        block = table[
            :,
            lax.div(time, slices),
            lax.div(op, ops),
            lax.rem(time, slices) * ops + lax.rem(op, ops),
        ]
        return block.astype(F32).reshape(columns, 2 * columns).astype(BF)

    pair_count = tau.shape[0]

    def one_pair(p, carry):
        total_real, total_imag = contract(
            entry(1, p), entry(0, p), tau, p, spin_signs, columns
        )
        partial[0, 0, pl.ds(p, 1), :] = jnp.sum(total_real, axis=0, keepdims=True)
        partial[0, 1, pl.ds(p, 1), :] = jnp.sum(total_imag, axis=0, keepdims=True)
        return carry

    lax.fori_loop(0, pair_count, one_pair, 0, unroll=True)
    p_copy = remote(partial.at[0], partial.at[1], p_send, p_recv, spin=1)
    p_copy.start()
    p_copy.wait_recv()
    c_out[...] = partial[0] + partial[1]
    p_copy.wait_send()
    for t in range(slices):
        halo_copy(t).wait_send()
        relay_copy(t).wait_send()
    for u in range(units):
        for d in range(1, layers):
            reduce_copy(u, d).wait_send()
            z_copy(u, d).wait_send()
        for d in range(layers):
            for e in range(times):
                if e:
                    t_copy(u, d, e).wait_send()
                c_copy(u, d, e).wait_send()


def last_kernel(blocks, sums, e_out, c_out):
    columns = e_out.shape[-1]
    for part in range(2):
        e_out[:, :, :, part, :] = blocks[:, :, :, part * columns : (part + 1) * columns]
        for p in range(sums.shape[1]):
            c_out[part, p] = jnp.sum(sums[part, p]) / (4.0 * columns)


def shards(eigvecs, links, directions, pair_list, pair_operators, perambulators):
    slices, _, _, local_sites, columns = eigvecs.shape
    sizes = {axis: lax.axis_size(axis) for axis in ("space", "tm", "spin")}
    layers, times, cores = sizes["space"], sizes["tm"], sizes["spin"]
    plane_count = local_sites // PLANE
    z_total = plane_count * layers
    scaling = 1.0 / math.sqrt(6.0 * PLANE * z_total)
    ops = directions.shape[0]
    rows = columns // layers
    pair_count = pair_list.shape[0]
    groups = local_sites // LANES
    units = slices * ops
    angles = 2.0 * np.pi / z_total * np.arange(z_total)
    phases = jnp.asarray(np.stack([np.cos(angles), np.sin(angles)]), F32)

    dma = pltpu.SemaphoreType.DMA
    vmem = pl.BlockSpec(memory_space=pltpu.VMEM)
    smem = pl.BlockSpec(memory_space=pltpu.SMEM)
    anywhere = pl.BlockSpec(memory_space=pl.ANY)
    by_link = jnp.transpose(links, (0, 1, 3, 4, 2, 5))
    by_plane = eigvecs.reshape(slices, 2, 3, plane_count, PLANE, columns)
    blocks, sums = pl.pallas_call(
        functools.partial(meson_kernel, sizes, slices, scaling),
        out_shape=(
            jax.ShapeDtypeStruct((slices, ops, rows, 2 * columns), F32),
            jax.ShapeDtypeStruct((2, pair_count, columns), F32),
        ),
        in_specs=[anywhere] * 7,
        out_specs=(vmem, vmem),
        scratch_shapes=[
            *[pltpu.VMEM((2, 3, 3 * plane_count + 1, PLANE, columns), BF) for _ in range(slices)],
            *[pltpu.VMEM((3, groups, 2 * columns, LANES), BF) for _ in range(ops)],
            pltpu.VMEM(by_link.shape, BF),
            pltpu.VMEM(perambulators.shape, BF),
            pltpu.VMEM((4, 27, local_sites), F32),
            pltpu.VMEM((2, 3, groups, columns, LANES), BF),
            pltpu.VMEM((units, layers, rows, 2 * columns), F32),
            pltpu.VMEM((units, layers - 1, rows, 2 * columns), F32),
            pltpu.VMEM((layers, times, cores, units, rows, 2 * columns), BF),
            pltpu.VMEM((2, 2, pair_count, columns), F32),
            dma((slices, plane_count)),
            dma((slices, 2)),
            dma(()),
            dma(()),
            dma((slices,)),
            dma((slices,)),
            dma((slices,)),
            dma((slices,)),
            dma((units, layers)),
            dma((units, layers)),
            dma((units, layers)),
            dma((units, layers)),
            dma((units, layers, times)),
            dma((units, layers, times)),
            dma((units, layers, times)),
            dma((units, layers, times)),
            dma(()),
            dma(()),
            pltpu.SMEM(directions.shape, jnp.int32),
            pltpu.SMEM((2, pair_count), jnp.int32),
            pltpu.SMEM((2, pair_count), jnp.int32),
            pltpu.SMEM(phases.shape, F32),
            dma((4,)),
        ],
        compiler_params=pltpu.CompilerParams(
            collective_id=0, has_side_effects=True, vmem_limit_bytes=56 << 20
        ),
        cost_estimate=pl.CostEstimate(
            flops=5_000_000_000, bytes_accessed=eigvecs.size * 2, transcendentals=0
        ),
        name="meson",
    )(directions, pair_list.T, pair_operators.T, phases, by_plane, by_link, perambulators)
    elementals, correlators = pl.pallas_call(
        last_kernel,
        out_shape=(
            jax.ShapeDtypeStruct((slices, ops, rows, 2, columns), F32),
            jax.ShapeDtypeStruct((2, pair_count), F32),
        ),
        in_specs=[vmem, vmem],
        out_specs=(vmem, smem),
        name="last",
    )(blocks, sums)
    return elementals, correlators.T


def solution(mesh):
    return jax.shard_map(
        shards,
        mesh=mesh,
        in_specs=(
            P("tm", None, None, "space", None),
            P("tm", None, None, None, None, "space"),
            P("spin"),
            P(("space", "tm"), None),
            P(("space", "tm"), None),
            P(("space", "tm"), "spin", None, None, None),
        ),
        out_specs=(P(("ens", "tm"), "spin", "space", None, None), P(("ens", "space", "tm"), None)),
        check_vma=False,
    )
```

```python
import functools
import math

import jax
import jax.numpy as jnp
import numpy as np
from jax import lax
from jax.experimental import pallas as pl
from jax.experimental.pallas import tpu as pltpu
from jax.sharding import PartitionSpec as P

PX = 16
PY = 16
PLANE = PX * PY
BF = jnp.bfloat16
F32 = jnp.float32
LANES = 128
WAIT = 6
MESH = pl.DeviceIdType.MESH


def fill_links(lk, links, phases, t, first_plane, plane_count):
    def keep(code, b, a, lanes, real, imag):
        for kind, value in enumerate((real, imag - real, imag + real)):
            lk[code, pl.ds(kind * 9 + b * 3 + a, 1), lanes] = value

    for code in range(3):
        for b in range(3):
            for a in range(3):
                pair = links[t, code, b, a].astype(F32)
                keep(code, b, a, slice(None), pair[0:1], pair[1:2])
    if t > 0:
        return
    for plane in range(plane_count):
        lanes = pl.ds(plane * PLANE, PLANE)
        for b in range(3):
            for a in range(3):
                real = phases[0, first_plane + plane] if a == b else 0.0
                imag = -phases[1, first_plane + plane] if a == b else 0.0
                keep(
                    3, b, a, lanes, jnp.full((1, PLANE), real, F32), jnp.full((1, PLANE), imag, F32)
                )


def stage_plane(work, turned, plane, plane_count):
    last = lax.broadcasted_iota(jnp.int32, (8, work.shape[-1]), 0) == 7
    along_x = 2 * plane_count + 1 + plane

    def group(g, carry):
        here = pl.ds(pl.multiple_of(g * PX, PX), PX)
        for part in range(2):
            for a in range(3):
                wide = work[part, a, plane, here, :].astype(F32)
                low, high = pltpu.roll(wide[:8], 7, 0), pltpu.roll(wide[8:], 7, 0)
                shifted = jnp.concatenate(
                    [jnp.where(last, high, low), jnp.where(last, low, high)], axis=0
                )
                work[part, a, along_x, here, :] = shifted.astype(BF)
        return carry

    lax.fori_loop(0, PY, group, 0, unroll=True)
    for part in range(2):
        for a in range(3):
            for s in range(PLANE // LANES):
                at = pl.ds(s * LANES, LANES)
                turned[part, a, plane * (PLANE // LANES) + s] = work[part, a, plane, at, :].T


def link_product(turned, lk, product, code, group):
    rows = 16
    columns = turned.shape[-2]
    lanes = pl.ds(pl.multiple_of(group * LANES, LANES), LANES)

    def link(kind, b, a):
        return jnp.broadcast_to(lk[code, pl.ds(kind * 9 + b * 3 + a, 1), lanes], (rows, LANES))

    u = [[[link(kind, b, a) for a in range(3)] for b in range(3)] for kind in range(3)]
    for first in range(0, columns, rows):
        real = [turned[0, b, group, pl.ds(first, rows), :].astype(F32) for b in range(3)]
        imag = [turned[1, b, group, pl.ds(first, rows), :].astype(F32) for b in range(3)]
        both = [real[b] + imag[b] for b in range(3)]

        def row(kind, a, field):
            return (
                u[kind][0][a] * field[0] + u[kind][1][a] * field[1] + u[kind][2][a] * field[2]
            )

        for a in range(3):
            common = row(0, a, both)
            out_real = common + row(1, a, imag)
            out_imag = common - row(2, a, real)
            product[a, group, pl.ds(first, rows), :] = out_real.astype(BF)
            product[a, group, pl.ds(columns + first, rows), :] = out_imag.astype(BF)


def gram(product, work, plane_count, offset):
    total = None
    for a in range(3):
        left = jnp.concatenate([product[a, s] for s in range(product.shape[1])], axis=1)
        right = jnp.concatenate(
            [
                jnp.concatenate([work[0, a, z + offset], work[1, a, z + offset]], axis=1)
                for z in range(plane_count)
            ],
            axis=0,
        )
        term = jnp.dot(left, right, preferred_element_type=F32)
        total = term if total is None else total + term
    return total


def contract(sink, source, tau, p, spin_signs, columns):
    sr, si = sink[:, :columns], sink[:, columns:]
    sink_block = jnp.concatenate(
        [jnp.concatenate([sr, -si], axis=1), jnp.concatenate([si, sr], axis=1)], axis=0
    )
    rr, ri = source[:, :columns], source[:, columns:]
    source_block = jnp.concatenate(
        [jnp.concatenate([rr, ri], axis=1), jnp.concatenate([-ri, rr], axis=1)], axis=0
    )
    total_real = jnp.zeros((8, columns), F32)
    total_imag = jnp.zeros((8, columns), F32)
    count = tau.shape[1]
    for first in range(0, count, 2):
        some = range(first, min(first + 2, count))
        stacked = jnp.concatenate(
            [jnp.concatenate([tau[p, q, 0], tau[p, q, 1]], axis=0) for q in some], axis=1
        )
        halfway = jnp.dot(sink_block, stacked, preferred_element_type=F32).astype(BF)
        lines = jnp.concatenate(
            [
                jnp.concatenate(
                    [
                        halfway[:columns, n * columns : (n + 1) * columns],
                        halfway[columns:, n * columns : (n + 1) * columns],
                    ],
                    axis=1,
                )
                for n in range(len(some))
            ],
            axis=0,
        )
        second = jnp.dot(lines, source_block, preferred_element_type=F32)
        for n, q in enumerate(some):
            out_real = second[n * columns : (n + 1) * columns, :columns]
            out_imag = second[n * columns : (n + 1) * columns, columns:]
            tau_real = tau[p, q, 0].astype(F32)
            tau_imag = tau[p, q, 1].astype(F32)
            real = out_real * tau_real + out_imag * tau_imag
            imag = out_imag * tau_real - out_real * tau_imag
            total_real += spin_signs[q] * jnp.sum(real.reshape(-1, 8, columns), axis=0)
            total_imag += spin_signs[q] * jnp.sum(imag.reshape(-1, 8, columns), axis=0)
    return total_real, total_imag


def meson_kernel(sizes, slices, scaling, *refs):
    scalars, (v_hbm, links_hbm, tau_hbm, e_out, c_out) = refs[:4], refs[4:9]
    dirs, pair_times, pair_ops, phases, scalar_sem = refs[-5:]
    works = refs[9 : 9 + slices]
    products = refs[9 + slices : 9 + slices + dirs.shape[0]]
    links, tau, lk, turned, own, held, table, partial = refs[9 + slices + dirs.shape[0] :][:8]
    (
        v_sem,
        y_sem,
        links_sem,
        tau_sem,
        halo_send,
        halo_recv,
        relay_send,
        relay_recv,
        r_send,
        r_recv,
        z_send,
        z_recv,
        t_send,
        t_recv,
        c_send,
        c_recv,
        p_send,
        p_recv,
    ) = refs[17 + slices + dirs.shape[0] : -5]
    layers, times, cores = sizes["space"], sizes["tm"], sizes["spin"]
    here = {axis: lax.axis_index(axis) for axis in sizes}
    plane_count, columns = v_hbm.shape[3], v_hbm.shape[5]
    ops = dirs.shape[0]
    groups = plane_count * (PLANE // LANES)
    rows = columns // layers
    units = slices * ops

    def local(src, dst, sem):
        return pltpu.make_async_copy(src, dst, sem)

    def target(**moves):
        return {axis: lax.rem(here[axis] + d, sizes[axis]) for axis, d in moves.items()}

    def remote(src, dst, send, recv, **moves):
        return pltpu.make_async_remote_copy(
            src_ref=src,
            dst_ref=dst,
            send_sem=send,
            recv_sem=recv,
            device_id=target(**moves),
            device_id_type=MESH,
        )

    def plane_copy(t, z):
        return local(v_hbm.at[t, :, :, z], works[t].at[:, :, z], v_sem.at[t, z])

    def y_copies(t):
        planes = pl.ds(plane_count + 1, plane_count)
        inner, edge = PLANE - PX, pl.ds(PLANE - PX, PX)
        return [
            local(
                v_hbm.at[t, :, :, :, pl.ds(PX, inner), :],
                works[t].at[:, :, planes, pl.ds(0, inner), :],
                y_sem.at[t, 0],
            ),
            local(
                v_hbm.at[t, :, :, :, pl.ds(0, PX), :],
                works[t].at[:, :, planes, edge, :],
                y_sem.at[t, 1],
            ),
        ]

    links_copy = local(links_hbm, links, links_sem)
    tau_copy = local(tau_hbm, tau, tau_sem)

    scalar_copies = [
        local(operand, held_as, scalar_sem.at[k])
        for k, (operand, held_as) in enumerate(zip(scalars, (dirs, pair_times, pair_ops, phases)))
    ]
    for copy in scalar_copies:
        copy.start()
    for z in range(plane_count):
        plane_copy(0, z).start()
    links_copy.start()

    barrier = pltpu.get_barrier_semaphore()
    for d, e in [(d, e) for d in range(layers) for e in range(times) if d or e]:
        pl.semaphore_signal(
            barrier, inc=1, device_id=target(space=d, tm=e), device_id_type=MESH
        )
    for f in range(1, cores):
        pl.semaphore_signal(barrier, inc=1, device_id=target(spin=f), device_id_type=MESH)

    core = here["spin"]

    def halo_copy(t):
        return remote(
            v_hbm.at[t, core, :, 0],
            works[t].at[core, :, plane_count],
            halo_send.at[t],
            halo_recv.at[t],
            space=layers - 1,
        )

    def relay_copy(t):
        plane = works[t].at[core, :, plane_count]
        return remote(plane, plane, relay_send.at[t], relay_recv.at[t], spin=1)

    def open_kernel(_):
        pl.semaphore_wait(barrier, layers * times + cores - 2)
        for t in range(slices):
            halo_copy(t).start()
        for copy in y_copies(0):
            copy.start()
        for t in range(1, slices):
            for z in range(plane_count):
                plane_copy(t, z).start()
            for copy in y_copies(t):
                copy.start()
        tau_copy.start()

    def reduce_copy(u, d):
        peer = lax.rem(here["space"] + d, layers)
        return remote(
            own.at[u, peer], held.at[u, d - 1], r_send.at[u, d], r_recv.at[u, d], space=d
        )

    far_first = sorted(range(1, layers), key=lambda d: abs(2 * d - layers))

    def finish_unit(u):
        code = dirs[u % ops]
        offset = jnp.where(
            code == 0,
            2 * plane_count + 1,
            jnp.where(code == 1, plane_count + 1, jnp.where(code == 2, 1, 0)),
        )
        value = gram(products[u % ops], works[u // ops], plane_count, offset)
        real = value[:columns, :columns] + value[columns:, columns:]
        imag = value[:columns, columns:] - value[columns:, :columns]
        straight = jnp.where(code == 3, scaling, 0.5 * scaling)
        crossed = jnp.where(code == 3, 0.0, 0.5 * scaling)
        whole = jnp.concatenate(
            [straight * real - crossed * real.T, straight * imag + crossed * imag.T], axis=1
        )
        own[u] = whole.reshape(layers, rows, 2 * columns)
        for d in far_first:
            reduce_copy(u, d).start()

    def slot(u, d, e):
        z = lax.rem(here["space"] + layers - d, layers)
        x = lax.rem(here["tm"] + times - e, times)
        return table.at[z, x, core, u]

    def z_copy(u, d):
        return remote(slot(u, 0, 0), slot(u, 0, 0), z_send.at[u, d], z_recv.at[u, d], space=d)

    def t_copy(u, d, e):
        sems = t_send.at[u, d, e], t_recv.at[u, d, e]
        if u == units - 1:
            return remote(slot(u, 0, 0), slot(u, 0, 0), *sems, space=d, tm=e)
        return remote(slot(u, d, 0), slot(u, d, 0), *sems, tm=e)

    def c_copy(u, d, e):
        block = slot(u, d, e)
        return remote(block, block, c_send.at[u, d, e], c_recv.at[u, d, e], spin=1)

    def start_times(u, d):
        for e in range(1, times):
            t_copy(u, d, e).start()

    def reduce_unit(u):
        total = own[u, here["space"]]
        for d in range(1, layers):
            reduce_copy(u, d).wait_recv()
            total += held[u, d - 1]
        e_out[u // ops, u % ops] = total
        table[here["space"], here["tm"], core, u] = total.astype(BF)
        if u == units - 1:
            for d in far_first:
                start_times(u, d)
                z_copy(u, d).start()
        else:
            for d in far_first:
                z_copy(u, d).start()
        start_times(u, 0)
        c_copy(u, 0, 0).start()

    def spread_layers(u):
        for d in range(1, layers):
            z_copy(u, d).wait_recv()
            if u < units - 1:
                start_times(u, d)
            c_copy(u, d, 0).start()

    def spread_times(u):
        for d in range(layers):
            for e in range(1, times):
                t_copy(u, d, e).wait_recv()
                c_copy(u, d, e).start()

    pending = []

    def tick():
        for entry in list(pending):
            entry[0] -= 1
            if entry[0] == 0:
                pending.remove(entry)
                entry[1](entry[2])

    def fetch_halo(t):
        halo_copy(t).wait_recv()
        relay_copy(t).start()

    def whole_slice(t):
        relay_copy(t).wait_recv()
        for copy in y_copies(t):
            copy.wait()

    def stage_slice(t):
        def stage(plane, carry):
            plane_copy(t, plane).wait()
            stage_plane(works[t], turned, plane, plane_count)
            return carry

        for half in range(2):
            lax.fori_loop(half * plane_count // 2, (half + 1) * plane_count // 2, stage, 0)
            tick()
        if t == 0:
            for copy in scalar_copies:
                copy.wait()
            links_copy.wait()
        fill_links(lk, links, phases, t, here["space"] * plane_count, plane_count)

    def link_unit(u):
        def group(g, carry):
            link_product(turned, lk, products[u % ops], dirs[u % ops], g)
            return carry

        for half in range(2):
            lax.fori_loop(half * groups // 2, (half + 1) * groups // 2, group, 0)
            tick()

    def close_unit(u):
        finish_unit(u)
        pending.append([WAIT, reduce_unit, u])
        pending.append([2 * WAIT, spread_layers, u])
        pending.append([(2 if u == units - 1 else 3) * WAIT, spread_times, u])
        tick()

    pending.append([1, open_kernel, None])
    stage_slice(0)
    for t in range(slices):
        first, last = t * ops, (t + 1) * ops - 1
        for u in range(first, last + 1):
            if t == 0 and u == last:
                pending.append([1, fetch_halo, t])
            if t > 0 and u == first:
                pending.append([1, fetch_halo, t])
            link_unit(u)
            if t > 0 and u < last:
                if u == first:
                    whole_slice(t)
                close_unit(u)
        if t == 0:
            whole_slice(t)
            for u in range(first, last):
                close_unit(u)
        if t + 1 < slices:
            stage_slice(t + 1)
        if t > 0 and first == last:
            whole_slice(t)
        close_unit(last)
    while pending:
        tick()
    tau_copy.wait()
    for u in range(units):
        for d in range(layers):
            for e in range(times):
                c_copy(u, d, e).wait_recv()

    count = tau.shape[1]
    spin_signs = []
    for q in range(count):
        pair = core * count + q
        same = (pair // 4 < 2) == (lax.rem(pair, 4) < 2)
        spin_signs.append(jnp.where(same, 1.0, -1.0))

    def entry(which, p):
        time, op = pair_times[which, p], pair_ops[which, p]
        block = table[
            :,
            lax.div(time, slices),
            lax.div(op, ops),
            lax.rem(time, slices) * ops + lax.rem(op, ops),
        ]
        if rows % 16 == 0:
            return jnp.concatenate([block[z] for z in range(layers)], axis=0)
        return block.astype(F32).reshape(columns, 2 * columns).astype(BF)

    pair_count = tau.shape[0]

    def one_pair(p, carry):
        total_real, total_imag = contract(
            entry(1, p), entry(0, p), tau, p, spin_signs, columns
        )
        partial[0, 0, pl.ds(p, 1), :] = jnp.sum(total_real, axis=0, keepdims=True)
        partial[0, 1, pl.ds(p, 1), :] = jnp.sum(total_imag, axis=0, keepdims=True)
        return carry

    lax.fori_loop(0, pair_count, one_pair, 0, unroll=True)
    p_copy = remote(partial.at[0], partial.at[1], p_send, p_recv, spin=1)
    p_copy.start()
    p_copy.wait_recv()
    c_out[...] = partial[0] + partial[1]
    p_copy.wait_send()
    for t in range(slices):
        halo_copy(t).wait_send()
        relay_copy(t).wait_send()
    for u in range(units):
        for d in range(1, layers):
            reduce_copy(u, d).wait_send()
            z_copy(u, d).wait_send()
        for d in range(layers):
            for e in range(times):
                if e:
                    t_copy(u, d, e).wait_send()
                c_copy(u, d, e).wait_send()


def last_kernel(blocks, sums, e_out, c_out):
    columns = e_out.shape[-1]
    for part in range(2):
        e_out[:, :, :, part, :] = blocks[:, :, :, part * columns : (part + 1) * columns]
        for p in range(sums.shape[1]):
            c_out[part, p] = jnp.sum(sums[part, p]) / (4.0 * columns)


def shards(eigvecs, links, directions, pair_list, pair_operators, perambulators):
    slices, _, _, local_sites, columns = eigvecs.shape
    sizes = {axis: lax.axis_size(axis) for axis in ("space", "tm", "spin")}
    layers, times, cores = sizes["space"], sizes["tm"], sizes["spin"]
    plane_count = local_sites // PLANE
    z_total = plane_count * layers
    scaling = 1.0 / math.sqrt(6.0 * PLANE * z_total)
    ops = directions.shape[0]
    rows = columns // layers
    pair_count = pair_list.shape[0]
    groups = local_sites // LANES
    units = slices * ops
    angles = 2.0 * np.pi / z_total * np.arange(z_total)
    phases = jnp.asarray(np.stack([np.cos(angles), np.sin(angles)]), F32)

    dma = pltpu.SemaphoreType.DMA
    vmem = pl.BlockSpec(memory_space=pltpu.VMEM)
    smem = pl.BlockSpec(memory_space=pltpu.SMEM)
    anywhere = pl.BlockSpec(memory_space=pl.ANY)
    by_link = jnp.transpose(links, (0, 1, 3, 4, 2, 5))
    by_plane = eigvecs.reshape(slices, 2, 3, plane_count, PLANE, columns)
    blocks, sums = pl.pallas_call(
        functools.partial(meson_kernel, sizes, slices, scaling),
        out_shape=(
            jax.ShapeDtypeStruct((slices, ops, rows, 2 * columns), F32),
            jax.ShapeDtypeStruct((2, pair_count, columns), F32),
        ),
        in_specs=[anywhere] * 7,
        out_specs=(vmem, vmem),
        scratch_shapes=[
            *[pltpu.VMEM((2, 3, 3 * plane_count + 1, PLANE, columns), BF) for _ in range(slices)],
            *[pltpu.VMEM((3, groups, 2 * columns, LANES), BF) for _ in range(ops)],
            pltpu.VMEM(by_link.shape, BF),
            pltpu.VMEM(perambulators.shape, BF),
            pltpu.VMEM((4, 27, local_sites), F32),
            pltpu.VMEM((2, 3, groups, columns, LANES), BF),
            pltpu.VMEM((units, layers, rows, 2 * columns), F32),
            pltpu.VMEM((units, layers - 1, rows, 2 * columns), F32),
            pltpu.VMEM((layers, times, cores, units, rows, 2 * columns), BF),
            pltpu.VMEM((2, 2, pair_count, columns), F32),
            dma((slices, plane_count)),
            dma((slices, 2)),
            dma(()),
            dma(()),
            dma((slices,)),
            dma((slices,)),
            dma((slices,)),
            dma((slices,)),
            dma((units, layers)),
            dma((units, layers)),
            dma((units, layers)),
            dma((units, layers)),
            dma((units, layers, times)),
            dma((units, layers, times)),
            dma((units, layers, times)),
            dma((units, layers, times)),
            dma(()),
            dma(()),
            pltpu.SMEM(directions.shape, jnp.int32),
            pltpu.SMEM((2, pair_count), jnp.int32),
            pltpu.SMEM((2, pair_count), jnp.int32),
            pltpu.SMEM(phases.shape, F32),
            dma((4,)),
        ],
        compiler_params=pltpu.CompilerParams(
            collective_id=0, has_side_effects=True, vmem_limit_bytes=56 << 20
        ),
        cost_estimate=pl.CostEstimate(
            flops=5_000_000_000, bytes_accessed=eigvecs.size * 2, transcendentals=0
        ),
        name="meson",
    )(directions, pair_list.T, pair_operators.T, phases, by_plane, by_link, perambulators)
    elementals, correlators = pl.pallas_call(
        last_kernel,
        out_shape=(
            jax.ShapeDtypeStruct((slices, ops, rows, 2, columns), F32),
            jax.ShapeDtypeStruct((2, pair_count), F32),
        ),
        in_specs=[vmem, vmem],
        out_specs=(vmem, smem),
        name="last",
    )(blocks, sums)
    return elementals, correlators.T


def solution(mesh):
    return jax.shard_map(
        shards,
        mesh=mesh,
        in_specs=(
            P("tm", None, None, "space", None),
            P("tm", None, None, None, None, "space"),
            P("spin"),
            P(("space", "tm"), None),
            P(("space", "tm"), None),
            P(("space", "tm"), "spin", None, None, None),
        ),
        out_specs=(P(("ens", "tm"), "spin", "space", None, None), P(("ens", "space", "tm"), None)),
        check_vma=False,
    )
```
